32 devices in a mesh: lat: 8 (over z, y), lon: 4 (over x, core).
Axes of the slice: x: 2, y: 2, z: 4, core: 2. Of those that a mesh axis runs over, the one named last changes fastest.
Arguments:
- features: bfloat16 [256, 16, 512], P(None, 'lat', 'lon'), may hold values from -6 to 6
- weight: bfloat16 [9, 65536], P(None, ('lat', 'lon')), may hold values from -0.125 to 0.125
- tap_values: bfloat16 [16, 5, 33], replicated, may hold values from -3 to 3
- basis_index: int32 [16, 5, 33], replicated, may hold values from 0 to 8
- half_width: int32 [16], replicated, may hold values from 1 to 16, as said below
- cotangent: bfloat16 [256, 16, 512], P(None, 'lat', 'lon'), may hold values from -6 to 6
Outputs:
- output: bfloat16 [256, 16, 512], P(None, 'lat', 'lon')
- input_grad: bfloat16 [256, 16, 512], P(None, 'lat', 'lon')
- weight_grad: float32 [9, 65536], P(None, ('lat', 'lon'))
The draws below stay inside these ranges and needn't reach their ends.
Inputs may be any that keep to these rules, and one draw needn't show every extreme that they name: `half_width`: the widest half-width is 16.
All inputs are finite; a program needn't handle non-finite values.
Results may differ from the reference program's by a relative error of at most 0.005.
Values may be sent and summed in bfloat16 or wider, within the bound.
No kernel may reach another device: no remote copies, remote signals or barrier semaphores. Data moves between devices by JAX's collectives and lax.ppermute only.
A program may use at most 64 MiB of HBM per device.

```python
import jax
import jax.numpy as jnp
from jax import lax

C = 256
K = 9
R = 2
HMAX = 16
NLAT = 16
NLON = 512


def draw_half_width(key, part):
    rows = jnp.arange(NLAT, dtype=jnp.int32)
    distance = jnp.abs(2 * rows + 1 - NLAT)
    base = 1 + (HMAX - 1) * distance * distance // ((NLAT - 1) * (NLAT - 1))
    jitter = jax.random.randint(key, (NLAT,), -1, 2, dtype=jnp.int32)
    widths = jnp.clip(base + jitter, 1, HMAX)
    return jnp.where(distance == NLAT - 1, HMAX, widths).astype(jnp.int32)


def set_ends(values, rng, smallest, high):
    longest = values.shape.index(max(values.shape))
    spots = []
    for shift in (0, 1):
        where = [jax.random.randint(jax.random.fold_in(rng, axis), (), 0, length) for axis, length in enumerate(values.shape)]
        where[longest] = (where[longest] + shift) % values.shape[longest]
        spots.append(tuple(where))
    return values.at[spots[0]].set(smallest).at[spots[1]].set(high)


def raised(entries, rng, source, target, blocks, factor):
    owner, partner = [(jnp.arange(entries.shape[dim]) // (entries.shape[dim] // blocks)).reshape([-1 if axis == dim else 1 for axis in range(entries.ndim)]) for dim in (source, target)]
    chosen = jax.random.permutation(rng, blocks)[partner]
    strong = (owner == chosen) | (owner == (partner + blocks // 2) % blocks)
    return jnp.where(strong, factor * entries, entries)


def shard_levels(own_key, dims, pieces, low, largest):
    def one(position, parts):
        draws = jax.random.uniform(jax.random.fold_in(jax.random.fold_in(own_key, 6), position), (parts,), jnp.float32, low / len(pieces), largest / len(pieces))
        return jnp.repeat(jnp.exp(draws), dims[position] // parts).reshape((-1,) + (1,) * (len(dims) - position - 1))

    loudness = one(*pieces[0])
    for cut in pieces[1:]:
        loudness = loudness * one(*cut)
    return loudness


def gaussian(rng, shape, scale, bound, pieces=(), kind=jnp.bfloat16):
    loudness = shard_levels(rng, shape, pieces, -0.22, 0.18) if pieces else 1.0
    values = jax.random.normal(rng, shape, jnp.float32) * scale * loudness
    return jnp.minimum(jnp.maximum(values, -bound), bound).astype(kind)


def gaussian_with(rng, dims, scale, limit, split, heavy, held_as=jnp.bfloat16):
    result = scale * jax.random.normal(rng, dims, jnp.float32)
    if split:
        result = result * shard_levels(rng, dims, split, -0.22, 0.18)
    return jnp.clip(raised(result, jax.random.fold_in(rng, 3), *heavy), -limit, limit).astype(held_as)


def setup_inputs(seed: int = 0) -> dict:
    key_list = jax.random.split(jax.random.key(seed), 7)
    return {
        "features": gaussian(key_list[0], (C, NLAT, NLON), 1.0, 6.0, ((1, 8), (2, 4))),
        "weight": gaussian(key_list[1], (K, C * C), (K * C) ** -0.5, 0.125, ((1, 32),)),
        "tap_values": gaussian(key_list[2], (NLAT, 2 * R + 1, 2 * HMAX + 1), 0.5, 3.0),
        "basis_index": set_ends(jax.random.randint(key_list[3], (NLAT, 2 * R + 1, 2 * HMAX + 1), 0, K), jax.random.fold_in(key_list[3], 1), 0, K - 1).astype(jnp.int32),
        "half_width": draw_half_width(jax.random.fold_in(key_list[6], 71), 0),
        "cotangent": gaussian_with(key_list[5], (C, NLAT, NLON), 1.0, 6.0, ((1, 8), (2, 4)), (1, 0, 8, 2.0)),
    }


def filters_of(tap_values, basis_index, half_width):
    offsets = jnp.abs(jnp.arange(2 * HMAX + 1) - HMAX)
    inside = offsets[None, None, :] <= half_width[:, None, None]
    kinds = jnp.arange(K)[:, None, None, None]
    chosen = (basis_index[None] == kinds) & inside[None]
    return jnp.where(chosen, tap_values[None], jnp.zeros((), tap_values.dtype))


def wrap_pad(field):
    padded = jnp.pad(field, ((0, 0), (R, R), (0, 0)))
    return jnp.concatenate([padded[:, :, NLON - HMAX:], padded, padded[:, :, :HMAX]], axis=2)


def reference(features, weight, tap_values, basis_index, half_width, cotangent):
    filters = filters_of(tap_values, basis_index, half_width)
    feat_pad = wrap_pad(features)
    weight_mat = weight.reshape(K * C, C)
    window = 2 * HMAX + 1

    def row_step(carry, row):
        grad_pad, weight_grad = carry
        rows_in = lax.dynamic_slice_in_dim(feat_pad, row, 2 * R + 1, axis=1)
        row_filters = lax.dynamic_slice_in_dim(filters, row, 1, axis=1)[:, 0].astype(jnp.float32)
        basis_sum = jnp.zeros((K, C, NLON), jnp.float32)
        for offset in range(2 * R + 1):
            source = rows_in[:, offset, :]
            windows = jnp.stack([source[:, shift:shift + NLON] for shift in range(window)], axis=1).astype(jnp.float32)
            basis_sum = basis_sum + jnp.einsum('cen,ke->kcn', windows, row_filters[:, offset, :])
        basis_out = basis_sum.astype(jnp.bfloat16).reshape(K * C, NLON)
        out_row = jnp.dot(weight_mat.T, basis_out, preferred_element_type=jnp.float32)
        grad_row = lax.dynamic_slice_in_dim(cotangent, row, 1, axis=1)[:, 0]
        weight_grad = weight_grad + jnp.dot(basis_out, grad_row.T, preferred_element_type=jnp.float32)
        basis_grad = jnp.dot(weight_mat, grad_row, preferred_element_type=jnp.float32).astype(jnp.bfloat16)
        basis_grad = basis_grad.reshape(K, C, NLON).astype(jnp.float32)
        for offset in range(2 * R + 1):
            spread = jnp.einsum('kcn,ke->ecn', basis_grad, row_filters[:, offset, :])
            line = jnp.zeros((C, NLON + 2 * HMAX), jnp.float32)
            for shift in range(window):
                line = line.at[:, shift:shift + NLON].add(spread[shift])
            current = lax.dynamic_slice_in_dim(grad_pad, row + offset, 1, axis=1)
            grad_pad = lax.dynamic_update_slice_in_dim(grad_pad, current + line[:, None, :], row + offset, axis=1)
        return (grad_pad, weight_grad), out_row.astype(jnp.bfloat16)

    start = (jnp.zeros((C, NLAT + 2 * R, NLON + 2 * HMAX), jnp.float32), jnp.zeros((K * C, C), jnp.float32))
    (grad_pad, weight_grad), out_rows = lax.scan(row_step, start, jnp.arange(NLAT, dtype=jnp.int32))
    output = jnp.transpose(out_rows, (1, 0, 2))
    core = grad_pad[:, R:R + NLAT, :]
    input_grad = core[:, :, HMAX:HMAX + NLON]
    input_grad = input_grad.at[:, :, NLON - HMAX:].add(core[:, :, :HMAX])
    input_grad = input_grad.at[:, :, :HMAX].add(core[:, :, HMAX + NLON:])
    return output, input_grad.astype(jnp.bfloat16), weight_grad.reshape(K, C * C)
```

```python
import jax
import jax.numpy as jnp
from jax import lax
from jax.experimental import pallas as pl
from jax.experimental.pallas import tpu as pltpu
from jax.sharding import PartitionSpec as P

TILE = 32
SLOT = 64
VMEM = 60 * 1024 * 1024
NT = (((1,), (1,)), ((), ()))
TN = (((0,), (0,)), ((), ()))


def dot(a, b, dims=(((1,), (0,)), ((), ()))):
    return lax.dot_general(a, b, dims, preferred_element_type=jnp.float32)


def in_vmem(count):
    return [pl.BlockSpec(memory_space=pltpu.VMEM) for _ in range(count)]


def call(body, outs, *args, scratch=()):
    return pl.pallas_call(
        body,
        out_shape=[jax.ShapeDtypeStruct(s, d) for s, d in outs],
        in_specs=in_vmem(len(args)),
        out_specs=in_vmem(len(outs)),
        scratch_shapes=list(scratch),
        compiler_params=pltpu.CompilerParams(vmem_limit_bytes=VMEM),
    )(*args)


def band_of(taps, index, basis_count):
    parts = []
    for basis in range(basis_count):
        line = jnp.where(index == basis, taps, 0.0)
        pieces = []
        for first in range(0, line.shape[1], 128):
            piece = jnp.broadcast_to(line[:, first : first + 128], (TILE, 128))
            pieces.append(pltpu.roll(piece, 0, 1, stride=1, stride_axis=0))
        parts.append(jnp.concatenate(pieces, axis=1).astype(jnp.bfloat16))
    return jnp.concatenate(parts, axis=0)


def convolve(source, taps_ref, index_ref, out_ref, rows, cols, offsets, basis_count):
    for row in range(rows):
        band = band_of(taps_ref[row], index_ref[row], basis_count)[:, : offsets * SLOT]
        for first in range(0, cols, TILE):
            lines = [source(row + a, first) for a in range(offsets)]
            moved = dot(band, jnp.concatenate(lines, axis=0)).astype(jnp.bfloat16)
            for basis in range(basis_count):
                start = row * cols + first
                out_ref[basis, start : start + TILE, :] = moved[basis * TILE : (basis + 1) * TILE]


def forward_body(ext_ref, perm_ref, taps_ref, index_ref, cot_ref, out_ref, send_ref, keep_ref, ext_scr):
    ext_rows, width, channels = ext_ref.shape
    basis_count = out_ref.shape[0]
    rows, cols = cot_ref.shape[0], cot_ref.shape[1]
    pick = (lax.broadcasted_iota(jnp.int32, (channels, channels), 0) == perm_ref[...]).astype(jnp.bfloat16)
    for row in range(ext_rows):
        ext_scr[row] = dot(ext_ref[row], pick).astype(jnp.bfloat16)
    convolve(
        lambda row, first: ext_scr[row, first : first + SLOT, :],
        taps_ref, index_ref, out_ref, rows, cols, ext_rows - rows + 1, basis_count,
    )
    cot = cot_ref[...].reshape(rows * cols, cot_ref.shape[2])
    half = channels // 2
    for basis in range(basis_count):
        terms = dot(out_ref[basis], cot, TN)
        send_ref[basis] = terms[half:].astype(send_ref.dtype)
        keep_ref[basis] = terms[:half]


def spread_body(ext_ref, taps_ref, index_ref, out_ref):
    ext_rows = ext_ref.shape[0]
    rows = taps_ref.shape[0]
    cols = out_ref.shape[1] // rows
    convolve(
        lambda row, first: ext_ref[row, first : first + SLOT, :],
        taps_ref, index_ref, out_ref, rows, cols, ext_rows - rows + 1, out_ref.shape[0],
    )


def mix_body(weight_ref, basis_ref, spread_ref, perm_ref, out_ref, grad_ref):
    basis_count, channels, _ = weight_ref.shape
    out = jnp.zeros(out_ref.shape[::-1], jnp.float32)
    grad = jnp.zeros(grad_ref.shape[::-1], jnp.float32)
    for basis in range(basis_count):
        out = out + dot(basis_ref[basis], weight_ref[basis])
        grad = grad + dot(spread_ref[basis], weight_ref[basis], NT)
    row = lax.broadcasted_iota(jnp.int32, (channels, channels), 0)
    col = lax.broadcasted_iota(jnp.int32, (channels, channels), 1)
    same = (row == col).astype(jnp.bfloat16)
    pick = (row == perm_ref[...]).astype(jnp.bfloat16)
    out_ref[...] = dot(same, out.astype(jnp.bfloat16), NT).astype(jnp.bfloat16)
    grad_ref[...] = dot(pick, grad.astype(jnp.bfloat16), NT).astype(jnp.bfloat16)


def swap(array, axis, stride):
    return lax.ppermute(array, axis, [(i, i ^ stride) for i in range(lax.axis_size(axis))])


def with_halo(array, axis, dim, width, wrap):
    devices, length = lax.axis_size(axis), array.shape[dim]
    up = [(i, (i + 1) % devices) for i in range(devices if wrap else devices - 1)]
    down = [(j, i) for i, j in up]
    before = lax.ppermute(lax.slice_in_dim(array, length - width, length, axis=dim), axis, up)
    after = lax.ppermute(lax.slice_in_dim(array, 0, width, axis=dim), axis, down)
    return jnp.concatenate([before, array, after], axis=dim)


def strides(axis):
    return [1 << b for b in range(lax.axis_size(axis).bit_length() - 1)]


def tap_lines(tap_values, basis_index, half_width, flip):
    lat_rows, offsets, window = tap_values.shape
    reach = (offsets - 1) // 2
    far = jnp.abs(jnp.arange(window) - (window - 1) // 2)
    index = jnp.where(far[None, None, :] <= half_width[:, None, None], basis_index, -1)
    taps = tap_values.astype(jnp.float32)
    if flip:
        pad = ((reach, reach), (0, 0), (0, 0))
        taps, index = jnp.pad(taps, pad), jnp.pad(index, pad, constant_values=-1)
        picked = [(a, offsets - 1 - a) for a in range(offsets)]
        taps = jnp.stack([taps[a : a + lat_rows, b, ::-1] for a, b in picked], axis=1)
        index = jnp.stack([index[a : a + lat_rows, b, ::-1] for a, b in picked], axis=1)
    slots = offsets + offsets % 2
    fill = ((0, 0), (0, slots - offsets), (0, SLOT - window))
    taps, index = jnp.pad(taps, fill), jnp.pad(index, fill, constant_values=-1)
    return taps.reshape(lat_rows, 1, slots * SLOT), index.reshape(lat_rows, 1, slots * SLOT)


def local(features, weight, tap_values, basis_index, half_width, cotangent):
    channels, lat_rows, lon_cols = features.shape
    basis_count = weight.shape[0]
    reach = (tap_values.shape[1] - 1) // 2
    rim = (tap_values.shape[2] - 1) // 2
    lats, lons = lax.axis_size("lat"), lax.axis_size("lon")
    devices = lats * lons
    parts = max(1, devices // channels)
    device = lax.axis_index("lat") * lons + lax.axis_index("lon")
    bf16 = jnp.bfloat16

    steps = [("lon", s, s) for s in strides("lon")] + [("lat", s, s * lons) for s in strides("lat")]
    split = [step for step in steps if step[2] < parts]
    steps = [step for step in steps if step[2] >= parts]
    own = channels * parts // devices
    place = jnp.arange(channels)
    perm = place % own + (device // parts) * own
    for rank, (_, _, bit) in enumerate(steps):
        size = channels >> (rank + 1)
        perm = perm ^ jnp.where(place & size, bit // parts * own, 0)
    perm = perm.astype(jnp.int32).reshape(1, channels)

    taps, index = tap_lines(tap_values, basis_index, half_width, False)
    flip_taps, flip_index = tap_lines(tap_values, basis_index, half_width, True)
    first = lax.axis_index("lat") * lat_rows
    taps, index, flip_taps, flip_index = (
        lax.dynamic_slice_in_dim(t, first, lat_rows, 0) for t in (taps, index, flip_taps, flip_index)
    )

    feat = jnp.transpose(features, (1, 2, 0))
    cot = jnp.transpose(cotangent, (1, 2, 0))
    feat_ext = with_halo(with_halo(feat, "lat", 0, reach, False), "lon", 1, rim, True)
    cot_ext = with_halo(with_halo(cot, "lat", 0, reach, False), "lon", 1, rim, True)

    full = weight.reshape(basis_count, own, channels // parts)
    for axis, stride, _ in split:
        other = swap(full, axis, stride)
        mine = (lax.axis_index(axis) // stride) % 2 == 0
        full = jnp.where(mine, jnp.concatenate([full, other], 2), jnp.concatenate([other, full], 2))
    for axis, stride, _ in reversed(steps):
        full = jnp.concatenate([full, swap(full, axis, stride)], axis=1)

    cells = lat_rows * lon_cols
    half = channels // 2
    basis_out, send, keep = call(
        forward_body,
        [((basis_count, cells, channels), bf16), ((basis_count, half, channels), jnp.float32),
         ((basis_count, half, channels), jnp.float32)],
        feat_ext, perm, taps, index, cot,
        scratch=[pltpu.VMEM(feat_ext.shape, bf16)],
    )
    for rank, (axis, stride, _) in enumerate(steps):
        terms = (keep, swap(send, axis, stride))
        if rank + 1 < len(steps):
            size = keep.shape[1] // 2
            send = terms[0][:, size:] + terms[1][:, size:]
            keep = terms[0][:, :size] + terms[1][:, :size]
    grad = terms[0] + terms[1]
    for axis, stride, _ in reversed(split):
        size = grad.shape[2] // 2
        mine = (lax.axis_index(axis) // stride) % 2
        other = swap(lax.dynamic_slice_in_dim(grad, (1 - mine) * size, size, 2), axis, stride)
        grad = lax.dynamic_slice_in_dim(grad, mine * size, size, 2) + other
    weight_grad = grad.reshape(basis_count, weight.shape[1])

    (spread,) = call(spread_body, [((basis_count, cells, channels), bf16)], cot_ext, flip_taps, flip_index)
    output, input_grad = call(
        mix_body, [((channels, cells), bf16), ((channels, cells), bf16)], full, basis_out, spread, perm
    )
    shape = (channels, lat_rows, lon_cols)
    return output.reshape(shape), input_grad.reshape(shape), weight_grad


def solution(mesh):
    field = P(None, "lat", "lon")
    flat = P(None, ("lat", "lon"))
    return jax.shard_map(
        local,
        mesh=mesh,
        in_specs=(field, flat, P(), P(), P(), field),
        out_specs=(field, field, flat),
        check_vma=False,
    )
```

```python
import jax
import jax.numpy as jnp
from jax import lax
from jax.experimental import pallas as pl
from jax.experimental.pallas import tpu as pltpu
from jax.sharding import PartitionSpec as P

TILE = 32
SLOT = 64
VMEM = 60 * 1024 * 1024
NT = (((1,), (1,)), ((), ()))
TN = (((0,), (0,)), ((), ()))
bf16, f32 = jnp.bfloat16, jnp.float32


def dot(a, b, dims=(((1,), (0,)), ((), ()))):
    return lax.dot_general(a, b, dims, preferred_element_type=f32)


def call(body, name, outs, *args, scratch=()):
    in_vmem = pl.BlockSpec(memory_space=pltpu.VMEM)
    return pl.pallas_call(
        body,
        name=name,
        out_shape=[jax.ShapeDtypeStruct(s, d) for s, d in outs],
        in_specs=[in_vmem for _ in args],
        out_specs=[in_vmem for _ in outs],
        scratch_shapes=list(scratch),
        compiler_params=pltpu.CompilerParams(vmem_limit_bytes=VMEM),
    )(*args)


def log2(size):
    return size.bit_length() - 1


class Layout:
    def __init__(self, channels, lats, lons):
        self.channels, self.lons = channels, lons
        devices = lats * lons
        self.parts = max(1, devices // channels)
        self.own = channels * self.parts // devices

        def bits(axis, size, scale):
            return [(axis, 1 << b, scale << b) for b in range(size.bit_length() - 1)]

        steps = bits("lon", lons, 1) + [s for s in bits("lat", lats, lons) if s[1] > 1]
        self.split = [s for s in steps if s[2] < self.parts]
        self.steps = [s for s in steps if s[2] >= self.parts]
        self.pair = lons // self.parts * self.own

    def odd(self):
        return lax.axis_index("lat") & 1

    def places(self, shape, dim):
        place = lax.broadcasted_iota(jnp.int32, shape, dim)
        device = lax.axis_index("lat") * self.lons + lax.axis_index("lon")
        channel = place & (self.own - 1)
        for rank, (_, _, bit) in enumerate(self.steps):
            value = bit // self.parts * self.own
            value = value // 2 if value > self.pair else value
            size = self.channels >> (rank + 2)
            differs = ((place >> log2(size)) ^ (device >> log2(bit))) & 1
            channel = channel + (differs << log2(value))
        return channel

    def whole(self, channel, odd):
        low = log2(self.pair)
        return ((channel >> low) << (low + 1)) + (odd << low) + (channel & (self.pair - 1))


def bands(taps_ref, index_ref, row, basis_count):
    taps, index = taps_ref[row], index_ref[row]

    def paired(v):
        return [jnp.concatenate([v[s : s + 1], v[s + 1 : s + 2]], axis=1) for s in range(0, v.shape[0], 2)]

    taps, index = paired(taps), paired(index)
    parts = []
    for basis in range(basis_count):
        pieces = []
        for line, kind in zip(taps, index):
            piece = jnp.broadcast_to(jnp.where(kind == basis, line, 0.0), (TILE, 2 * SLOT))
            pieces.append(pltpu.roll(piece, 0, 1, stride=1, stride_axis=0))
        parts.append(jnp.concatenate(pieces, axis=1).astype(bf16))
    return jnp.concatenate(parts, axis=0)


def place_rows(scr, move, own_ref, pair_ref, near_ref, next_ref, core_ref, cross_ref):
    rows, cols = own_ref.shape[0], own_ref.shape[1]
    rim = core_ref.shape[1]
    odd, flip = lax.axis_index("lat") & 1, (lax.axis_index("lat") >> 1) & 1
    even_col = (lax.axis_index("lon") & 1) == 0
    slots = ((1 - flip) * 3 * rows, (1 + odd) * rows, (2 - odd) * rows, flip * 3 * rows)
    for rank, (slot, ref) in enumerate(zip(slots, (near_ref, own_ref, pair_ref, next_ref))):
        for row in range(rows):
            core, cross = core_ref[rank * rows + row], cross_ref[rank * rows + row]
            scr[slot + row, rim : rim + cols, :] = move(ref[row])
            scr[slot + row, :rim, :] = move(jnp.where(even_col, cross, core))
            scr[slot + row, rim + cols :, :] = move(jnp.where(even_col, core, cross))


def forward_body(lay, offsets, own_ref, pair_ref, near_ref, next_ref, core_ref, cross_ref, taps_ref, index_ref,
                 own_cot_ref, pair_cot_ref, out_ref, send_ref, keep_ref, ext_scr):
    rows, cols, channels = own_ref.shape
    basis_count = out_ref.shape[0]
    odd = lay.odd()
    shape = (channels, channels)
    pick = (lax.broadcasted_iota(jnp.int32, shape, 0) == lay.places(shape, 1)).astype(bf16)
    place_rows(ext_scr, lambda v: dot(v, pick).astype(bf16), own_ref, pair_ref, near_ref, next_ref, core_ref, cross_ref)
    first_row = (lax.axis_index("lat") - odd) * rows
    for line in range(2 * rows):
        low = (odd if line < rows else 1 - odd) * rows + line % rows
        band = bands(taps_ref, index_ref, first_row + low + rows, basis_count)[:, : offsets * SLOT]
        for first in range(0, cols, 2 * TILE):
            source = [
                jnp.concatenate([ext_scr[low + a, start : start + SLOT, :] for a in range(offsets)], axis=0)
                for start in (first, first + TILE)
            ]
            moved = dot(band, jnp.concatenate(source, axis=1)).astype(bf16)
            for basis in range(basis_count):
                for side in range(2):
                    start = line * cols + first + side * TILE
                    piece = moved[basis * TILE : (basis + 1) * TILE, side * channels : (side + 1) * channels]
                    out_ref[basis, start : start + TILE, :] = piece
    cot = jnp.concatenate([own_cot_ref[...], pair_cot_ref[...]], axis=0).reshape(2 * rows * cols, own_cot_ref.shape[2])
    half = channels // 2
    for basis in range(basis_count):
        terms = dot(out_ref[basis], cot, TN)
        send_ref[basis] = terms[half:].astype(send_ref.dtype)
        keep_ref[basis] = terms[:half]


def mix_body(weight_ref, basis_ref, own_ref, pair_ref):
    basis_count, channels, outs = weight_ref.shape
    cells = own_ref.shape[0]
    source = jnp.concatenate([basis_ref[basis] for basis in range(basis_count)], axis=1)
    total = dot(source, weight_ref[...].reshape(basis_count * channels, outs))
    own_ref[...] = total[:cells]
    pair_ref[...] = total[cells:]


def backward_body(lay, offsets, own_ref, pair_ref, near_ref, next_ref, core_ref, cross_ref, taps_ref, index_ref,
                  weight_ref, own_grad_ref, pair_grad_ref, ext_scr, basis_scr, sum_scr):
    rows, cols, _ = own_ref.shape
    basis_count, channels, outs = weight_ref.shape
    odd = lay.odd()
    place_rows(ext_scr, lambda v: v, own_ref, pair_ref, near_ref, next_ref, core_ref, cross_ref)
    weight = weight_ref[...].reshape(basis_count * channels, outs)
    first_row = (lax.axis_index("lat") - odd) * rows
    ext_rows, ext_cols, _ = ext_scr.shape
    reach, blocks = offsets // 2, ext_cols // TILE
    sum_scr[...] = jnp.zeros(sum_scr.shape, f32)
    for row in range(ext_rows):
        basis_grad = dot(ext_scr[row], weight, NT).astype(bf16)
        for basis in range(basis_count):
            for block in range(blocks):
                piece = basis_grad[block * TILE : (block + 1) * TILE, basis * channels : (basis + 1) * channels]
                side = block % 2 * channels
                basis_scr[block // 2, basis * TILE : (basis + 1) * TILE, side : side + channels] = piece
        wanted = [a for a in range(offsets) if rows <= row + a - reach < 3 * rows]
        low = wanted[0] // 2 * 2
        high = min(wanted[-1] // 2 * 2 + 2, offsets)
        band = bands(taps_ref, index_ref, first_row + row, basis_count)[:, low * SLOT : high * SLOT]
        for block in range(0, blocks, 2):
            sides = min(2, blocks - block)
            spread = dot(band, basis_scr[block // 2, :, : sides * channels], TN)
            for a in wanted:
                for side in range(sides):
                    target, start = row + a - reach - rows, (block + side) * TILE
                    piece = spread[(a - low) * SLOT : (a - low + 1) * SLOT, side * channels : (side + 1) * channels]
                    sum_scr[target, start : start + SLOT, :] = sum_scr[target, start : start + SLOT, :] + piece
    for row in range(rows):
        for ref, slot in ((own_grad_ref, odd * rows), (pair_grad_ref, (1 - odd) * rows)):
            ref[row * cols : (row + 1) * cols, :] = sum_scr[slot + row, TILE : TILE + cols, :].astype(bf16)


def finish_body(lay, own_ref, pair_ref, grad_ref):
    shape = (own_ref.shape[1], grad_ref.shape[1])
    place, column = lay.places(shape, 0), lax.broadcasted_iota(jnp.int32, shape, 1)
    odd = lay.odd()
    own = (column == lay.whole(place, odd)).astype(bf16)
    pair = (column == lay.whole(place, 1 - odd)).astype(bf16)
    grad_ref[...] = (dot(own_ref[...], own) + dot(pair_ref[...], pair)).astype(bf16)


def swap(array, axis, stride):
    return lax.ppermute(array, axis, [(i, i ^ stride) for i in range(lax.axis_size(axis))])


def swap_across(array, axis, stride, wrap):
    size = lax.axis_size(axis)
    pairs = [(i, i + stride if i // stride % 2 else i - stride) for i in range(size)]
    return lax.ppermute(array, axis, [(i, j % size) for i, j in pairs if wrap or 0 <= j < size])


def around(own, pair, rim):
    lat, lon = lax.axis_index("lat"), lax.axis_index("lon")
    own_first = (lat & 1) != ((lat >> 1) & 1)
    near = swap(jnp.where(own_first, own, pair), "lat", 2)
    far = swap_across(jnp.where(own_first, pair, own), "lat", 2, False)
    lines = (near, own, pair, far)
    first = jnp.concatenate([v[:, :rim] for v in lines], axis=0)
    last = jnp.concatenate([v[:, -rim:] for v in lines], axis=0)
    even = (lon & 1) == 0
    core = swap(jnp.where(even, last, first), "lon", 1)
    cross = swap_across(jnp.where(even, first, last), "lon", 1, True)
    return near, far, core, cross


def local(features, weight, tap_values, basis_index, half_width, cotangent):
    channels, rows, cols = features.shape
    basis_count = weight.shape[0]
    _, offsets, window = tap_values.shape
    rim = (window - 1) // 2
    lay = Layout(channels, lax.axis_size("lat"), lax.axis_size("lon"))
    odd = lay.odd()
    half = channels // 2

    split = features.reshape(half // lay.pair, 2, lay.pair, rows, cols)
    to_pair = lax.dynamic_index_in_dim(split, 1 - odd, 1, False).reshape(half, rows, cols)
    to_keep = lax.dynamic_index_in_dim(split, odd, 1, False).reshape(half, rows, cols)
    feat_pair = jnp.transpose(swap(to_pair, "lat", 1), (1, 2, 0))
    feat_own = jnp.transpose(to_keep, (1, 2, 0))
    cot_pair = jnp.transpose(swap(cotangent, "lat", 1), (1, 2, 0))
    cot_own = jnp.transpose(cotangent, (1, 2, 0))

    far = jnp.abs(jnp.arange(window) - rim)
    index = jnp.where(far[None, None, :] <= half_width[:, None, None], basis_index, -1)
    fill = ((rows, rows), (0, offsets % 2), (0, SLOT - window))
    index = jnp.pad(index, fill, constant_values=-1)
    taps = jnp.pad(tap_values.astype(f32), fill)

    feat_around = around(feat_own, feat_pair, rim)
    cot_around = around(cot_own, cot_pair, rim)

    full = weight.reshape(basis_count, lay.own, channels // lay.parts)
    for axis, stride, _ in lay.split:
        other = swap(full, axis, stride)
        low = (lax.axis_index(axis) // stride) % 2 == 0
        full = jnp.where(low, jnp.concatenate([full, other], 2), jnp.concatenate([other, full], 2))
    for axis, stride, _ in reversed(lay.steps):
        full = jnp.concatenate([full, swap(full, axis, stride)], axis=1)

    cells = rows * cols
    ext = (4 * rows, cols + 2 * rim)
    basis_out, send, keep = call(
        lambda *refs: forward_body(lay, offsets, *refs), "forward",
        [((basis_count, 2 * cells, half), bf16), ((basis_count, half // 2, channels), f32),
         ((basis_count, half // 2, channels), f32)],
        feat_own, feat_pair, *feat_around, taps, index, cot_own, cot_pair,
        scratch=[pltpu.VMEM((*ext, half), bf16)],
    )
    for rank, (axis, stride, _) in enumerate(lay.steps):
        terms = (keep, swap(send, axis, stride))
        if rank + 1 < len(lay.steps):
            size = keep.shape[1] // 2
            send = terms[0][:, size:] + terms[1][:, size:]
            keep = terms[0][:, :size] + terms[1][:, :size]
    grad = terms[0] + terms[1]
    for axis, stride, _ in reversed(lay.split):
        size = grad.shape[2] // 2
        mine = (lax.axis_index(axis) // stride) % 2
        other = swap(lax.dynamic_slice_in_dim(grad, (1 - mine) * size, size, 2), axis, stride)
        grad = lax.dynamic_slice_in_dim(grad, mine * size, size, 2) + other
    weight_grad = grad.reshape(basis_count, weight.shape[1])

    own_out, pair_out = call(mix_body, "mix", [((cells, channels), f32), ((cells, channels), f32)], full, basis_out)
    pair_out = swap(pair_out, "lat", 1)
    own_grad, pair_grad = call(
        lambda *refs: backward_body(lay, offsets, *refs), "backward",
        [((cells, half), bf16), ((cells, half), bf16)],
        cot_own, cot_pair, *cot_around, taps, index, full,
        scratch=[pltpu.VMEM((*ext, channels), bf16),
                 pltpu.VMEM((-(-ext[1] // (2 * TILE)), basis_count * TILE, 2 * half), bf16),
                 pltpu.VMEM((2 * rows, ext[1] + TILE, half), f32)],
    )
    pair_grad = swap(pair_grad, "lat", 1)
    output = (own_out + pair_out).astype(bf16)
    (input_grad,) = call(
        lambda *refs: finish_body(lay, *refs), "finish", [((cells, channels), bf16)], own_grad, pair_grad
    )

    def channels_first(v):
        return jnp.transpose(v.reshape(rows, cols, channels), (2, 0, 1))

    return channels_first(output), channels_first(input_grad), weight_grad


def solution(mesh):
    field = P(None, "lat", "lon")
    flat = P(None, ("lat", "lon"))
    return jax.shard_map(
        local,
        mesh=mesh,
        in_specs=(field, flat, P(), P(), P(), field),
        out_specs=(field, field, flat),
        check_vma=False,
    )
```

```python
import jax
import jax.numpy as jnp
from jax import lax
from jax.experimental import pallas as pl
from jax.experimental.pallas import tpu as pltpu
from jax.sharding import PartitionSpec as P

TILE = 32
SLOT = 64
VMEM = 16 * 1024 * 1024
NT = (((1,), (1,)), ((), ()))
TN = (((0,), (0,)), ((), ()))
bf16, f32 = jnp.bfloat16, jnp.float32


def dot(a, b, dims=(((1,), (0,)), ((), ()))):
    return lax.dot_general(a, b, dims, preferred_element_type=f32)


def call(body, name, outs, *args, scratch=()):
    in_vmem = pl.BlockSpec(memory_space=pltpu.VMEM)
    return pl.pallas_call(
        body,
        name=name,
        out_shape=[jax.ShapeDtypeStruct(s, d) for s, d in outs],
        in_specs=[in_vmem for _ in args],
        out_specs=[in_vmem for _ in outs],
        scratch_shapes=list(scratch),
        compiler_params=pltpu.CompilerParams(vmem_limit_bytes=VMEM),
    )(*args)


def log2(size):
    return size.bit_length() - 1


class Layout:
    def __init__(self, channels, lats, lons):
        self.channels, self.lons = channels, lons
        devices = lats * lons
        self.parts = max(1, devices // channels)
        self.own = channels * self.parts // devices

        def bits(axis, size, scale):
            return [(axis, 1 << b, scale << b) for b in range(size.bit_length() - 1)]

        steps = bits("lon", lons, 1) + [s for s in bits("lat", lats, lons) if s[1] > 1]
        self.split = [s for s in steps if s[2] < self.parts]
        self.steps = [s for s in steps if s[2] >= self.parts]
        self.pair = lons // self.parts * self.own

    def odd(self):
        return lax.axis_index("lat") & 1

    def places(self, shape, dim):
        place = lax.broadcasted_iota(jnp.int32, shape, dim)
        device = lax.axis_index("lat") * self.lons + lax.axis_index("lon")
        channel = place & (self.own - 1)
        for rank, (_, _, bit) in enumerate(self.steps):
            value = bit // self.parts * self.own
            value = value // 2 if value > self.pair else value
            size = self.channels >> (rank + 2)
            differs = ((place >> log2(size)) ^ (device >> log2(bit))) & 1
            channel = channel + (differs << log2(value))
        return channel

    def whole(self, channel, odd):
        low = log2(self.pair)
        return ((channel >> low) << (low + 1)) + (odd << low) + (channel & (self.pair - 1))


def bands(taps_ref, index_ref, row, basis_count):
    taps, index = taps_ref[row], index_ref[row]

    def paired(v):
        return [jnp.concatenate([v[s : s + 1], v[s + 1 : s + 2]], axis=1) for s in range(0, v.shape[0], 2)]

    taps, index = paired(taps), paired(index)
    parts = []
    for basis in range(basis_count):
        pieces = []
        for line, kind in zip(taps, index):
            piece = jnp.broadcast_to(jnp.where(kind == basis, line, 0.0), (TILE, 2 * SLOT))
            pieces.append(pltpu.roll(piece, 0, 1, stride=1, stride_axis=0))
        parts.append(jnp.concatenate(pieces, axis=1).astype(bf16))
    return jnp.concatenate(parts, axis=0)


def place_rows(scr, move, own_ref, pair_ref, near_ref, next_ref, core_ref, cross_ref):
    rows, cols = own_ref.shape[0], own_ref.shape[1]
    rim = core_ref.shape[1]
    odd, flip = lax.axis_index("lat") & 1, (lax.axis_index("lat") >> 1) & 1
    even_col = (lax.axis_index("lon") & 1) == 0
    slots = ((1 - flip) * 3 * rows, (1 + odd) * rows, (2 - odd) * rows, flip * 3 * rows)
    for rank, (slot, ref) in enumerate(zip(slots, (near_ref, own_ref, pair_ref, next_ref))):
        for row in range(rows):
            core, cross = core_ref[rank * rows + row], cross_ref[rank * rows + row]
            scr[slot + row, rim : rim + cols, :] = move(ref[row])
            scr[slot + row, :rim, :] = move(jnp.where(even_col, cross, core))
            scr[slot + row, rim + cols :, :] = move(jnp.where(even_col, core, cross))


def forward_body(lay, offsets, own_ref, pair_ref, near_ref, next_ref, core_ref, cross_ref, taps_ref, index_ref,
                 own_cot_ref, pair_cot_ref, out_ref, send_ref, keep_ref, ext_scr):
    rows, cols, channels = own_ref.shape
    basis_count = out_ref.shape[0]
    odd = lay.odd()
    shape = (channels, channels)
    pick = (lax.broadcasted_iota(jnp.int32, shape, 0) == lay.places(shape, 1)).astype(bf16)
    place_rows(ext_scr, lambda v: dot(v, pick).astype(bf16), own_ref, pair_ref, near_ref, next_ref, core_ref, cross_ref)
    first_row = (lax.axis_index("lat") - odd) * rows
    for line in range(2 * rows):
        low = (odd if line < rows else 1 - odd) * rows + line % rows
        band = bands(taps_ref, index_ref, first_row + low + rows, basis_count)[:, : offsets * SLOT]
        for first in range(0, cols, 2 * TILE):
            source = [
                jnp.concatenate([ext_scr[low + a, start : start + SLOT, :] for a in range(offsets)], axis=0)
                for start in (first, first + TILE)
            ]
            moved = dot(band, jnp.concatenate(source, axis=1)).astype(bf16)
            for basis in range(basis_count):
                for side in range(2):
                    start = line * cols + first + side * TILE
                    piece = moved[basis * TILE : (basis + 1) * TILE, side * channels : (side + 1) * channels]
                    out_ref[basis, start : start + TILE, :] = piece
    cot = jnp.concatenate([own_cot_ref[...], pair_cot_ref[...]], axis=0).reshape(2 * rows * cols, own_cot_ref.shape[2])
    half = channels // 2
    for basis in range(basis_count):
        terms = dot(out_ref[basis], cot, TN)
        send_ref[basis] = terms[half:].astype(send_ref.dtype)
        keep_ref[basis] = terms[:half]


def mix_body(weight_ref, basis_ref, own_ref, pair_ref):
    basis_count, channels, outs = weight_ref.shape
    cells = own_ref.shape[0]
    source = jnp.concatenate([basis_ref[basis] for basis in range(basis_count)], axis=1)
    total = dot(source, weight_ref[...].reshape(basis_count * channels, outs))
    own_ref[...] = total[:cells]
    pair_ref[...] = total[cells:]


def backward_body(lay, offsets, own_ref, pair_ref, near_ref, next_ref, core_ref, cross_ref, taps_ref, index_ref,
                  weight_ref, own_grad_ref, pair_grad_ref, ext_scr, basis_scr, sum_scr):
    rows, cols, _ = own_ref.shape
    basis_count, channels, outs = weight_ref.shape
    odd = lay.odd()
    place_rows(ext_scr, lambda v: v, own_ref, pair_ref, near_ref, next_ref, core_ref, cross_ref)
    weight = weight_ref[...].reshape(basis_count * channels, outs)
    first_row = (lax.axis_index("lat") - odd) * rows
    ext_rows, ext_cols, _ = ext_scr.shape
    reach, blocks = offsets // 2, ext_cols // TILE
    sum_scr[...] = jnp.zeros(sum_scr.shape, f32)
    for row in range(ext_rows):
        basis_grad = dot(ext_scr[row], weight, NT).astype(bf16)
        for basis in range(basis_count):
            for block in range(blocks):
                piece = basis_grad[block * TILE : (block + 1) * TILE, basis * channels : (basis + 1) * channels]
                side = block % 2 * channels
                basis_scr[block // 2, basis * TILE : (basis + 1) * TILE, side : side + channels] = piece
        wanted = [a for a in range(offsets) if rows <= row + a - reach < 3 * rows]
        low = wanted[0] // 2 * 2
        high = min(wanted[-1] // 2 * 2 + 2, offsets)
        band = bands(taps_ref, index_ref, first_row + row, basis_count)[:, low * SLOT : high * SLOT]
        for block in range(0, blocks, 2):
            sides = min(2, blocks - block)
            spread = dot(band, basis_scr[block // 2, :, : sides * channels], TN)
            for a in wanted:
                for side in range(sides):
                    target, start = row + a - reach - rows, (block + side) * TILE
                    piece = spread[(a - low) * SLOT : (a - low + 1) * SLOT, side * channels : (side + 1) * channels]
                    sum_scr[target, start : start + SLOT, :] = sum_scr[target, start : start + SLOT, :] + piece
    for row in range(rows):
        for ref, slot in ((own_grad_ref, odd * rows), (pair_grad_ref, (1 - odd) * rows)):
            ref[row * cols : (row + 1) * cols, :] = sum_scr[slot + row, TILE : TILE + cols, :].astype(bf16)


def finish_body(lay, own_ref, pair_ref, grad_ref):
    shape = (own_ref.shape[1], grad_ref.shape[1])
    place, column = lay.places(shape, 0), lax.broadcasted_iota(jnp.int32, shape, 1)
    odd = lay.odd()
    own = (column == lay.whole(place, odd)).astype(bf16)
    pair = (column == lay.whole(place, 1 - odd)).astype(bf16)
    grad_ref[...] = (dot(own_ref[...], own) + dot(pair_ref[...], pair)).astype(bf16)


def after(array, *others):
    return lax.optimization_barrier((array, *others))[0]


def swap(array, axis, stride):
    return lax.ppermute(array, axis, [(i, i ^ stride) for i in range(lax.axis_size(axis))])


def swap_across(array, axis, stride, wrap):
    size = lax.axis_size(axis)
    pairs = [(i, i + stride if i // stride % 2 else i - stride) for i in range(size)]
    return lax.ppermute(array, axis, [(i, j % size) for i, j in pairs if wrap or 0 <= j < size])


def row_halo(own, pair):
    lat = lax.axis_index("lat")
    own_first = (lat & 1) != ((lat >> 1) & 1)
    near = swap(jnp.where(own_first, own, pair), "lat", 2)
    far = swap_across(jnp.where(own_first, pair, own), "lat", 2, False)
    return near, far


def edges(lines, rim):
    first = jnp.concatenate([v[:, :rim] for v in lines], axis=0)
    last = jnp.concatenate([v[:, -rim:] for v in lines], axis=0)
    even = (lax.axis_index("lon") & 1) == 0
    return jnp.where(even, last, first), jnp.where(even, first, last)


def column_halo(to_core, to_cross):
    return swap(to_core, "lon", 1), swap_across(to_cross, "lon", 1, True)


def local(features, weight, tap_values, basis_index, half_width, cotangent):
    channels, rows, cols = features.shape
    basis_count = weight.shape[0]
    _, offsets, window = tap_values.shape
    rim = (window - 1) // 2
    lay = Layout(channels, lax.axis_size("lat"), lax.axis_size("lon"))
    odd = lay.odd()
    half = channels // 2

    split = features.reshape(half // lay.pair, 2, lay.pair, rows, cols)
    to_pair = lax.dynamic_index_in_dim(split, 1 - odd, 1, False).reshape(half, rows, cols)
    to_keep = lax.dynamic_index_in_dim(split, odd, 1, False).reshape(half, rows, cols)
    feat_pair = jnp.transpose(swap(to_pair, "lat", 1), (1, 2, 0))
    feat_own = jnp.transpose(to_keep, (1, 2, 0))
    cot_pair = jnp.transpose(swap(cotangent, "lat", 1), (1, 2, 0))
    cot_own = jnp.transpose(cotangent, (1, 2, 0))

    far = jnp.abs(jnp.arange(window) - rim)
    index = jnp.where(far[None, None, :] <= half_width[:, None, None], basis_index, -1)
    fill = ((rows, rows), (0, offsets % 2), (0, SLOT - window))
    index = jnp.pad(index, fill, constant_values=-1)
    taps = jnp.pad(tap_values.astype(f32), fill)

    near, far = row_halo(feat_own, feat_pair)
    full = weight.reshape(basis_count, lay.own, channels // lay.parts)
    for axis, stride, _ in lay.split:
        other = swap(full, axis, stride)
        low = (lax.axis_index(axis) // stride) % 2 == 0
        full = jnp.where(low, jnp.concatenate([full, other], 2), jnp.concatenate([other, full], 2))
    gather = list(reversed(lay.steps))

    def widen(full, step):
        return jnp.concatenate([full, swap(full, step[0], step[1])], axis=1)

    full = widen(full, gather[0])
    full = widen(after(full, feat_pair), gather[1])
    to_core, to_cross = edges((near, feat_own, feat_pair, far), rim)
    feat_around = (near, far, *column_halo(to_core, to_cross))
    full = after(full, to_core, to_cross)
    for step in gather[2:-1]:
        full = widen(full, step)

    cells = rows * cols
    ext = (4 * rows, cols + 2 * rim)
    basis_out, send, keep = call(
        lambda *refs: forward_body(lay, offsets, *refs), "forward",
        [((basis_count, 2 * cells, half), bf16), ((basis_count, half // 2, channels), f32),
         ((basis_count, half // 2, channels), f32)],
        feat_own, feat_pair, *feat_around, taps, index, cot_own, cot_pair,
        scratch=[pltpu.VMEM((*ext, half), bf16)],
    )
    cot_near, cot_far = row_halo(after(cot_own, send), after(cot_pair, send))
    full = widen(after(full, send), gather[-1])
    sent = [send]
    for rank, (axis, stride, _) in enumerate(lay.steps):
        terms = (keep, swap(send, axis, stride))
        if rank + 1 < len(lay.steps):
            size = keep.shape[1] // 2
            send = terms[0][:, size:] + terms[1][:, size:]
            keep = terms[0][:, :size] + terms[1][:, :size]
            sent.append(send)
    grad = terms[0] + terms[1]
    for axis, stride, _ in reversed(lay.split):
        size = grad.shape[2] // 2
        mine = (lax.axis_index(axis) // stride) % 2
        other = swap(lax.dynamic_slice_in_dim(grad, (1 - mine) * size, size, 2), axis, stride)
        grad = lax.dynamic_slice_in_dim(grad, mine * size, size, 2) + other
    weight_grad = grad.reshape(basis_count, weight.shape[1])

    cot_around = (cot_near, cot_far, *column_halo(*edges((cot_near, cot_own, cot_pair, cot_far), rim)))
    own_out, pair_out = call(mix_body, "mix", [((cells, channels), f32), ((cells, channels), f32)], full, basis_out)
    own_grad, pair_grad = call(
        lambda *refs: backward_body(lay, offsets, *refs), "backward",
        [((cells, half), bf16), ((cells, half), bf16)],
        after(cot_own, pair_out, sent[-2]), cot_pair, *cot_around, taps, index, full,
        scratch=[pltpu.VMEM((*ext, channels), bf16),
                 pltpu.VMEM((-(-ext[1] // (2 * TILE)), basis_count * TILE, 2 * half), bf16),
                 pltpu.VMEM((2 * rows, ext[1] + TILE, half), f32)],
    )
    pair_out = swap(pair_out, "lat", 1)
    pair_grad = swap(pair_grad, "lat", 1)
    output = (own_out + pair_out).astype(bf16)
    (input_grad,) = call(
        lambda *refs: finish_body(lay, *refs), "finish", [((cells, channels), bf16)], own_grad, pair_grad
    )

    def channels_first(v):
        return jnp.transpose(v.reshape(rows, cols, channels), (2, 0, 1))

    return channels_first(output), channels_first(input_grad), weight_grad


def solution(mesh):
    field = P(None, "lat", "lon")
    flat = P(None, ("lat", "lon"))
    return jax.shard_map(
        local,
        mesh=mesh,
        in_specs=(field, flat, P(), P(), P(), field),
        out_specs=(field, field, flat),
        check_vma=False,
    )
```

```python
import jax
import jax.numpy as jnp
from jax import lax
from jax.experimental import pallas as pl
from jax.experimental.pallas import tpu as pltpu
from jax.sharding import PartitionSpec as P

TILE = 32
SLOT = 64
VMEM = 16 * 1024 * 1024
NT = (((1,), (1,)), ((), ()))
TN = (((0,), (0,)), ((), ()))
bf16, f32 = jnp.bfloat16, jnp.float32


def dot(a, b, dims=(((1,), (0,)), ((), ()))):
    return lax.dot_general(a, b, dims, preferred_element_type=f32)


def call(body, name, flops, outs, *args, scratch=()):
    in_vmem = pl.BlockSpec(memory_space=pltpu.VMEM)
    return pl.pallas_call(
        body,
        name=name,
        out_shape=[jax.ShapeDtypeStruct(s, d) for s, d in outs],
        in_specs=[in_vmem for _ in args],
        out_specs=[in_vmem for _ in outs],
        scratch_shapes=list(scratch),
        cost_estimate=pl.CostEstimate(
            flops=flops, transcendentals=0, bytes_accessed=sum(v.size * v.dtype.itemsize for v in args)
        ),
        compiler_params=pltpu.CompilerParams(vmem_limit_bytes=VMEM),
    )(*args)


def log2(size):
    return size.bit_length() - 1


class Layout:
    def __init__(self, channels, lats, lons):
        self.channels, self.lons = channels, lons
        devices = lats * lons
        self.parts = max(1, devices // channels)
        self.own = channels * self.parts // devices
        self.bits = [1 << b for b in range(devices.bit_length() - 1) if 1 << b != lons]
        self.merged = lats == 8 and lons == 4 and self.parts == 1
        if self.merged:
            steps = [("lon", 1), ("lat", 2), ("lon", 3), ("lat", 4)]
        else:
            steps = [("lon", 1 << b) for b in range(lons.bit_length() - 1)]
            steps += [("lat", 2 << b) for b in range(lats.bit_length() - 2)]
        steps = [(axis, flip, flip if axis == "lon" else flip * lons) for axis, flip in steps]
        self.split = [s for s in steps if s[2] < self.parts]
        self.steps = [s for s in steps if s[2] >= self.parts]
        self.pair = lons // self.parts * self.own

    def odd(self):
        return lax.axis_index("lat") & 1

    def places(self, shape, dim):
        place = lax.broadcasted_iota(jnp.int32, shape, dim)
        owner = lax.axis_index("lat") * self.lons + lax.axis_index("lon")
        for rank, (_, _, flip) in enumerate(self.steps):
            owner = owner ^ (((place >> log2(self.channels >> (rank + 2))) & 1) * flip)
        channel = place & (self.own - 1)
        for bit in self.bits:
            if bit >= self.parts:
                value = bit // self.parts * self.own
                value = value // 2 if value > self.pair else value
                channel = channel + (((owner >> log2(bit)) & 1) << log2(value))
        return channel

    def whole(self, channel, odd):
        low = log2(self.pair)
        return ((channel >> low) << (low + 1)) + (odd << low) + (channel & (self.pair - 1))


def bands(taps_ref, index_ref, row, basis_count, picked, offsets):
    taps, index = taps_ref[row], index_ref[row]

    def line(v, a, none):
        return v[a : a + 1] if 0 <= a < offsets else jnp.full((1, SLOT), none, v.dtype)

    def paired(v, none):
        return [
            jnp.concatenate([line(v, a, none), line(v, b, none)], axis=1)
            for a, b in zip(picked[::2], picked[1::2] + [-1] * (len(picked) % 2))
        ]

    taps, index = paired(taps, 0.0), paired(index, -1)
    parts = []
    for basis in range(basis_count):
        pieces = []
        for value, kind in zip(taps, index):
            piece = jnp.broadcast_to(jnp.where(kind == basis, value, 0.0), (TILE, 2 * SLOT))
            pieces.append(pltpu.roll(piece, 0, 1, stride=1, stride_axis=0))
        parts.append(jnp.concatenate(pieces, axis=1).astype(bf16))
    return jnp.concatenate(parts, axis=0)


def place_rows(scr, move, own_ref, pair_ref, near_ref, next_ref, core_ref, cross_ref):
    rows, cols, channels = own_ref.shape
    lat, lon = lax.axis_index("lat"), lax.axis_index("lon")
    odd, flip = lat & 1, (lat >> 1) & 1
    even_col = (lon & 1) == 0
    rim = (scr.shape[1] - cols) // 2
    wide = near_ref.shape[1] // channels

    def part(ref, first, row, length):
        low = (first + row // wide) * length
        return ref[low : low + length, row % wide * channels : (row % wide + 1) * channels]

    slots = ((1 - flip) * 3 * rows, (1 + odd) * rows, (2 - odd) * rows, flip * 3 * rows)
    for rank, slot in enumerate(slots):
        for row in range(rows):
            line = part((near_ref, next_ref)[rank // 3], 0, row, cols) if rank in (0, 3) else (own_ref, pair_ref)[rank - 1][row]
            core = part(core_ref, rank * (rows // wide), row, rim)
            cross = part(cross_ref, rank * (rows // wide), row, rim)
            scr[slot + row, rim : rim + cols, :] = move(line)
            scr[slot + row, :rim, :] = move(jnp.where(even_col, cross, core))
            scr[slot + row, rim + cols :, :] = move(jnp.where(even_col, core, cross))


def forward_body(lay, offsets, own_ref, pair_ref, near_ref, next_ref, core_ref, cross_ref, taps_ref, index_ref,
                 own_cot_ref, pair_cot_ref, out_ref, send_ref, keep_ref, ext_scr):
    rows, cols, channels = own_ref.shape
    basis_count = out_ref.shape[0]
    odd = lay.odd()
    shape = (channels, channels)
    pick = (lax.broadcasted_iota(jnp.int32, shape, 0) == lay.places(shape, 1)).astype(bf16)
    place_rows(ext_scr, lambda v: dot(v, pick).astype(bf16), own_ref, pair_ref, near_ref, next_ref, core_ref, cross_ref)
    first_row = (lax.axis_index("lat") - odd) * rows
    for line in range(2 * rows):
        low = (odd if line < rows else 1 - odd) * rows + line % rows
        picked = list(range(offsets))
        band = bands(taps_ref, index_ref, first_row + low + rows, basis_count, picked, offsets)[:, : offsets * SLOT]
        for first in range(0, cols, 2 * TILE):
            source = [
                jnp.concatenate([ext_scr[low + a, start : start + SLOT, :] for a in range(offsets)], axis=0)
                for start in (first, first + TILE)
            ]
            moved = dot(band, jnp.concatenate(source, axis=1)).astype(bf16)
            for basis in range(basis_count):
                for side in range(2):
                    start = line * cols + first + side * TILE
                    piece = moved[basis * TILE : (basis + 1) * TILE, side * channels : (side + 1) * channels]
                    out_ref[basis, start : start + TILE, :] = piece
    cot = jnp.concatenate([own_cot_ref[...], pair_cot_ref[...]], axis=0).reshape(2 * rows * cols, own_cot_ref.shape[2])
    half = channels // 2
    for basis in range(basis_count):
        terms = dot(out_ref[basis], cot, TN)
        send_ref[basis] = terms[half:].astype(send_ref.dtype)
        keep_ref[basis] = terms[:half]


def mix_body(weight_ref, basis_ref, own_ref, pair_ref):
    basis_count, channels, outs = weight_ref.shape
    cells = own_ref.shape[0]
    source = jnp.concatenate([basis_ref[basis] for basis in range(basis_count)], axis=1)
    total = dot(source, weight_ref[...].reshape(basis_count * channels, outs))
    own_ref[...] = total[:cells]
    pair_ref[...] = total[cells:].astype(pair_ref.dtype)


def backward_body(lay, offsets, own_ref, pair_ref, near_ref, next_ref, core_ref, cross_ref, taps_ref, index_ref,
                  weight_ref, own_grad_ref, pair_grad_ref, ext_scr, basis_scr, band_scr, sum_scr):
    rows, cols, _ = own_ref.shape
    basis_count, channels, outs = weight_ref.shape
    odd = lay.odd()
    place_rows(ext_scr, lambda v: v, own_ref, pair_ref, near_ref, next_ref, core_ref, cross_ref)
    weight = weight_ref[...].reshape(basis_count * channels, outs)
    first_row = (lax.axis_index("lat") - odd) * rows
    ext_rows, ext_cols, _ = ext_scr.shape
    blocks = ext_cols // TILE
    for row in range(ext_rows):
        basis_grad = dot(ext_scr[row], weight, NT).astype(bf16)
        low = row * basis_count * TILE
        for basis in range(basis_count):
            for block in range(blocks):
                piece = basis_grad[block * TILE : (block + 1) * TILE, basis * channels : (basis + 1) * channels]
                start = low + basis * TILE
                basis_scr[start : start + TILE, block * channels : (block + 1) * channels] = piece
        reached = [target + 2 * (offsets // 2) - row for target in range(2 * rows)]
        band_scr[low : low + basis_count * TILE, :] = bands(taps_ref, index_ref, first_row + row, basis_count, reached, offsets)
    sum_scr[...] = jnp.zeros(sum_scr.shape, f32)
    for block in range(0, blocks, 2):
        sides = min(2, blocks - block)
        spread = dot(band_scr[...], basis_scr[:, block * channels : (block + sides) * channels], TN)
        for target in range(2 * rows):
            for side in range(sides):
                start = (block + side) * TILE
                piece = spread[target * SLOT : (target + 1) * SLOT, side * channels : (side + 1) * channels]
                sum_scr[target, start : start + SLOT, :] = sum_scr[target, start : start + SLOT, :] + piece
    for row in range(rows):
        for ref, slot in ((own_grad_ref, odd * rows), (pair_grad_ref, (1 - odd) * rows)):
            ref[row * cols : (row + 1) * cols, :] = sum_scr[slot + row, TILE : TILE + cols, :].astype(bf16)


def finish_body(lay, own_ref, pair_ref, grad_ref):
    shape = (own_ref.shape[1], grad_ref.shape[1])
    place, column = lay.places(shape, 0), lax.broadcasted_iota(jnp.int32, shape, 1)
    odd = lay.odd()
    own = (column == lay.whole(place, odd)).astype(bf16)
    pair = (column == lay.whole(place, 1 - odd)).astype(bf16)
    grad_ref[...] = (dot(own_ref[...], own) + dot(pair_ref[...], pair)).astype(bf16)


def after(array, *others):
    return lax.optimization_barrier((array, *others))[0]


def swap(array, axis, stride):
    return lax.ppermute(array, axis, [(i, i ^ stride) for i in range(lax.axis_size(axis))])


def swap_across(array, axis, stride, wrap):
    size = lax.axis_size(axis)
    pairs = [(i, i + stride if i // stride % 2 else i - stride) for i in range(size)]
    return lax.ppermute(array, axis, [(i, j % size) for i, j in pairs if wrap or 0 <= j < size])


def flat(rows, width):
    wide = width // rows.shape[2]
    lines = [
        jnp.concatenate([rows[row + side] for side in range(wide)], axis=1) for row in range(0, rows.shape[0], wide)
    ]
    return jnp.concatenate(lines, axis=0)


def row_halo(own, pair, width, near_more):
    lat = lax.axis_index("lat")
    own_first = (lat & 1) != ((lat >> 1) & 1)
    to_near, to_far = jnp.where(own_first, own, pair), jnp.where(own_first, pair, own)
    near = swap(jnp.concatenate([flat(to_near, width), *near_more], axis=0), "lat", 2)
    return near, swap_across(flat(to_far, width), "lat", 2, False)


def edges(near, own, pair, far, rim, width):
    rows, cols, channels = own.shape
    lines = rows * channels // width

    def at(first):
        def halo(v):
            return [v[line * cols + first : line * cols + first + rim] for line in range(lines)]

        kept = [flat(v[:, first : first + rim], width) for v in (own, pair)]
        return jnp.concatenate([*halo(near), *kept, *halo(far)], axis=0)

    even = (lax.axis_index("lon") & 1) == 0
    left, right = at(0), at(cols - rim)
    return jnp.where(even, right, left), jnp.where(even, left, right)


def column_halo(lay, to_core, to_cross, cross_more):
    to_cross = jnp.concatenate([to_cross, *cross_more], axis=0)
    cross = swap(to_cross, "lon", 3) if lay.merged else swap_across(to_cross, "lon", 1, True)
    return swap(to_core, "lon", 1), cross


def local(features, weight, tap_values, basis_index, half_width, cotangent):
    channels, rows, cols = features.shape
    basis_count = weight.shape[0]
    _, offsets, window = tap_values.shape
    rim = (window - 1) // 2
    lay = Layout(channels, lax.axis_size("lat"), lax.axis_size("lon"))
    odd = lay.odd()
    half = channels // 2

    split = features.reshape(half // lay.pair, 2, lay.pair, rows, cols)
    to_pair = lax.dynamic_index_in_dim(split, 1 - odd, 1, False).reshape(half, rows, cols)
    to_keep = lax.dynamic_index_in_dim(split, odd, 1, False).reshape(half, rows, cols)
    feat_pair = jnp.transpose(swap(to_pair, "lat", 1), (1, 2, 0))
    feat_own = jnp.transpose(to_keep, (1, 2, 0))
    cot_pair = jnp.transpose(swap(cotangent, "lat", 1), (1, 2, 0))
    cot_own = jnp.transpose(cotangent, (1, 2, 0))

    far = jnp.abs(jnp.arange(window) - rim)
    index = jnp.where(far[None, None, :] <= half_width[:, None, None], basis_index, -1)
    fill = ((rows, rows), (0, offsets % 2), (0, SLOT - window))
    index = jnp.pad(index, fill, constant_values=-1)
    taps = jnp.pad(tap_values.astype(f32), fill)

    full = weight.reshape(basis_count, lay.own, channels // lay.parts)
    for axis, flip, _ in lay.split:
        other = swap(full, axis, flip)
        low = (lax.axis_index(axis) // flip) % 2 == 0
        full = jnp.where(low, jnp.concatenate([full, other], 2), jnp.concatenate([other, full], 2))
    gather = list(reversed(lay.steps))

    def widen(full, step):
        return jnp.concatenate([full, swap(full, step[0], step[1])], axis=1)

    lot = basis_count * lay.own

    def tail(array, count):
        return [array[array.shape[0] - (i + 1) * lot : array.shape[0] - i * lot] for i in reversed(range(count))]

    own, by_next = [], []
    if lay.merged:
        own = [after(weight, to_pair).reshape(lot, channels)]
        own = [lax.optimization_barrier(own[0])]
        by_next = [swap(own[0], "lat", 4)]
    near, far = row_halo(feat_own, feat_pair, channels, own)
    by_near = tail(near, len(own))
    to_core, to_cross = edges(near, feat_own, feat_pair, far, rim, channels)
    core, cross = column_halo(lay, to_core, to_cross, own + by_next + by_near)
    if not lay.merged:
        for step in gather[:-1]:
            full = widen(full, step)
    cot_near, cot_far = row_halo(after(cot_own, to_core, to_cross), cot_pair, channels, by_next)

    cells = rows * cols
    ext = (4 * rows, cols + 2 * rim)
    basis_out, send, keep = call(
        lambda *refs: forward_body(lay, offsets, *refs), "forward", 16 * basis_count * cells * half * channels,
        [((basis_count, 2 * cells, half), bf16), ((basis_count, half // 2, channels), f32),
         ((basis_count, half // 2, channels), f32)],
        feat_own, feat_pair, near, far, core, cross, taps, index, cot_own, cot_pair,
        scratch=[pltpu.VMEM((*ext, half), bf16)],
    )
    for rank, (axis, flip, _) in enumerate(lay.steps):
        terms = (keep, swap(send, axis, flip))
        if rank == 0:
            cot_near, cot_far = after(cot_near, send), after(cot_far, send)
        elif rank == 1:
            by_both = tail(cot_near, len(own))
            to_core, to_cross = edges(cot_near, cot_own, cot_pair, cot_far, rim, channels)
            to_core, to_cross = after(to_core, send), after(to_cross, send)
            cot_core, cot_cross = column_halo(lay, to_core, to_cross, by_both)
        elif rank == 2:
            cot_core, cot_cross = after(cot_core, send), after(cot_cross, send)
            cot_around = (cot_near, cot_far, cot_core, cot_cross)
            if lay.merged:
                here, there = own + by_next + by_near + by_both, tail(cross, 3) + tail(cot_cross, 1)
                held = here[:2] + there[:2] + here[2:] + there[2:]
                full = jnp.concatenate([v.reshape(basis_count, lay.own, channels) for v in held], axis=1)
            full = widen(full, gather[-1])
            own_out, pair_out = call(
                mix_body, "mix", 4 * basis_count * cells * half * channels, [((cells, channels), f32), ((cells, channels), bf16)], full, basis_out
            )
            cot_after = after(cot_own, pair_out)
            pair_out = swap(pair_out, "lat", 1)
            cot_around = (cot_near, cot_far, cot_core, cot_cross)
            own_grad, pair_grad = call(
                lambda *refs: backward_body(lay, offsets, *refs), "backward", 48 * basis_count * cells * half * channels,
                [((cells, half), bf16), ((cells, half), bf16)],
                cot_after, cot_pair, *cot_around, taps, index, full,
                scratch=[pltpu.VMEM((*ext, channels), bf16),
                         pltpu.VMEM((ext[0] * basis_count * TILE, ext[1] // TILE * half), bf16),
                         pltpu.VMEM((ext[0] * basis_count * TILE, 2 * rows * SLOT), bf16),
                         pltpu.VMEM((2 * rows, ext[1] + TILE, half), f32)],
            )
            pair_grad = swap(pair_grad, "lat", 1)
        if rank + 1 < len(lay.steps):
            size = keep.shape[1] // 2
            send = (terms[0][:, size:] + terms[1][:, size:]).astype(bf16 if rank < 2 else f32)
            keep = terms[0][:, :size] + terms[1][:, :size]
        if rank == 2:
            send = after(send, own_grad)
    grad = terms[0] + terms[1]
    for axis, flip, _ in reversed(lay.split):
        size = grad.shape[2] // 2
        odd_part = (lax.axis_index(axis) // flip) % 2
        other = swap(lax.dynamic_slice_in_dim(grad, (1 - odd_part) * size, size, 2), axis, flip)
        grad = lax.dynamic_slice_in_dim(grad, odd_part * size, size, 2) + other
    weight_grad = grad.reshape(basis_count, weight.shape[1])

    output = (own_out + pair_out).astype(bf16)
    (input_grad,) = call(
        lambda *refs: finish_body(lay, *refs), "finish", 4 * cells * half * channels, [((cells, channels), bf16)], own_grad, pair_grad
    )

    def channels_first(v):
        return jnp.transpose(v.reshape(rows, cols, channels), (2, 0, 1))

    return channels_first(output), channels_first(input_grad), weight_grad


def solution(mesh):
    field = P(None, "lat", "lon")
    flat = P(None, ("lat", "lon"))
    return jax.shard_map(
        local,
        mesh=mesh,
        in_specs=(field, flat, P(), P(), P(), field),
        out_specs=(field, field, flat),
        check_vma=False,
    )
```

```python
import jax
import jax.numpy as jnp
from jax import lax
from jax.experimental import pallas as pl
from jax.experimental.pallas import tpu as pltpu
from jax.sharding import PartitionSpec as P

TILE = 32
SLOT = 64
VMEM = 16 * 1024 * 1024
NT = (((1,), (1,)), ((), ()))
TN = (((0,), (0,)), ((), ()))
bf16, f32 = jnp.bfloat16, jnp.float32


def dot(a, b, dims=(((1,), (0,)), ((), ()))):
    return lax.dot_general(a, b, dims, preferred_element_type=f32)


def call(body, name, flops, outs, *args, scratch=()):
    in_vmem = pl.BlockSpec(memory_space=pltpu.VMEM)
    return pl.pallas_call(
        body,
        name=name,
        out_shape=[jax.ShapeDtypeStruct(s, d) for s, d in outs],
        in_specs=[in_vmem for _ in args],
        out_specs=[in_vmem for _ in outs],
        scratch_shapes=list(scratch),
        cost_estimate=pl.CostEstimate(
            flops=flops, transcendentals=0, bytes_accessed=sum(v.size * v.dtype.itemsize for v in args)
        ),
        compiler_params=pltpu.CompilerParams(vmem_limit_bytes=VMEM),
    )(*args)


def log2(size):
    return size.bit_length() - 1


class Layout:
    def __init__(self, channels, lats, lons):
        self.channels, self.lons = channels, lons
        devices = lats * lons
        self.parts = max(1, devices // channels)
        self.own = channels * self.parts // devices
        self.bits = [1 << b for b in range(devices.bit_length() - 1) if 1 << b != lons]
        self.merged = lats == 8 and lons == 4 and self.parts == 1
        if self.merged:
            steps = [("lon", 1), ("lat", 2), ("lon", 3), ("lat", 4)]
        else:
            steps = [("lon", 1 << b) for b in range(lons.bit_length() - 1)]
            steps += [("lat", 2 << b) for b in range(lats.bit_length() - 2)]
        steps = [(axis, flip, flip if axis == "lon" else flip * lons) for axis, flip in steps]
        self.split = [s for s in steps if s[2] < self.parts]
        self.steps = [s for s in steps if s[2] >= self.parts]
        self.pair = lons // self.parts * self.own

    def odd(self):
        return lax.axis_index("lat") & 1

    def places(self, shape, dim):
        place = lax.broadcasted_iota(jnp.int32, shape, dim)
        owner = lax.axis_index("lat") * self.lons + lax.axis_index("lon")
        for rank, (_, _, flip) in enumerate(self.steps):
            owner = owner ^ (((place >> log2(self.channels >> (rank + 2))) & 1) * flip)
        channel = place & (self.own - 1)
        for bit in self.bits:
            if bit >= self.parts:
                value = bit // self.parts * self.own
                value = value // 2 if value > self.pair else value
                channel = channel + (((owner >> log2(bit)) & 1) << log2(value))
        return channel

    def whole(self, channel, odd):
        low = log2(self.pair)
        return ((channel >> low) << (low + 1)) + (odd << low) + (channel & (self.pair - 1))


def bands(taps_ref, index_ref, row, basis_count, picked, offsets):
    taps, index = taps_ref[row], index_ref[row]

    def line(v, a, none):
        return v[a : a + 1] if 0 <= a < offsets else jnp.full((1, SLOT), none, v.dtype)

    def paired(v, none):
        return [
            jnp.concatenate([line(v, a, none), line(v, b, none)], axis=1)
            for a, b in zip(picked[::2], picked[1::2] + [-1] * (len(picked) % 2))
        ]

    taps, index = paired(taps, 0.0), paired(index, -1)
    parts = []
    for basis in range(basis_count):
        pieces = []
        for value, kind in zip(taps, index):
            piece = jnp.broadcast_to(jnp.where(kind == basis, value, 0.0), (TILE, 2 * SLOT))
            pieces.append(pltpu.roll(piece, 0, 1, stride=1, stride_axis=0))
        parts.append(jnp.concatenate(pieces, axis=1).astype(bf16))
    return jnp.concatenate(parts, axis=0)


def place_rows(scr, move, own_ref, pair_ref, near_ref, next_ref, core_ref, cross_ref):
    rows, cols, channels = own_ref.shape
    lat, lon = lax.axis_index("lat"), lax.axis_index("lon")
    odd, flip = lat & 1, (lat >> 1) & 1
    even_col = (lon & 1) == 0
    rim = (scr.shape[1] - cols) // 2
    wide = near_ref.shape[1] // channels

    def part(ref, first, row, length):
        low = (first + row // wide) * length
        return ref[low : low + length, row % wide * channels : (row % wide + 1) * channels]

    slots = ((1 - flip) * 3 * rows, (1 + odd) * rows, (2 - odd) * rows, flip * 3 * rows)
    for rank, slot in enumerate(slots):
        for row in range(rows):
            line = part((near_ref, next_ref)[rank // 3], 0, row, cols) if rank in (0, 3) else (own_ref, pair_ref)[rank - 1][row]
            core = part(core_ref, rank * (rows // wide), row, rim)
            cross = part(cross_ref, rank * (rows // wide), row, rim)
            scr[slot + row, rim : rim + cols, :] = move(line)
            scr[slot + row, :rim, :] = move(jnp.where(even_col, cross, core))
            scr[slot + row, rim + cols :, :] = move(jnp.where(even_col, core, cross))


def forward_body(lay, offsets, own_ref, pair_ref, near_ref, next_ref, core_ref, cross_ref, taps_ref, index_ref,
                 own_cot_ref, pair_cot_ref, out_ref, send_ref, keep_ref, ext_scr):
    rows, cols, channels = own_ref.shape
    basis_count = out_ref.shape[0]
    odd = lay.odd()
    shape = (channels, channels)
    pick = (lax.broadcasted_iota(jnp.int32, shape, 0) == lay.places(shape, 1)).astype(bf16)
    place_rows(ext_scr, lambda v: dot(v, pick).astype(bf16), own_ref, pair_ref, near_ref, next_ref, core_ref, cross_ref)
    first_row = (lax.axis_index("lat") - odd) * rows
    for line in range(2 * rows):
        low = (odd if line < rows else 1 - odd) * rows + line % rows
        picked = list(range(offsets))
        band = bands(taps_ref, index_ref, first_row + low + rows, basis_count, picked, offsets)[:, : offsets * SLOT]
        for first in range(0, cols, 2 * TILE):
            source = [
                jnp.concatenate([ext_scr[low + a, start : start + SLOT, :] for a in range(offsets)], axis=0)
                for start in (first, first + TILE)
            ]
            moved = dot(band, jnp.concatenate(source, axis=1)).astype(bf16)
            for basis in range(basis_count):
                for side in range(2):
                    start = line * cols + first + side * TILE
                    piece = moved[basis * TILE : (basis + 1) * TILE, side * channels : (side + 1) * channels]
                    out_ref[basis, start : start + TILE, :] = piece
    cot = jnp.concatenate([own_cot_ref[...], pair_cot_ref[...]], axis=0).reshape(2 * rows * cols, own_cot_ref.shape[2])
    half = channels // 2
    for basis in range(basis_count):
        terms = dot(out_ref[basis], cot, TN)
        send_ref[basis] = terms[half:].astype(send_ref.dtype)
        keep_ref[basis] = terms[:half]


def mix_body(weight_ref, basis_ref, own_ref, pair_ref):
    basis_count, channels, outs = weight_ref.shape
    cells = own_ref.shape[0]
    source = jnp.concatenate([basis_ref[basis] for basis in range(basis_count)], axis=1)
    total = dot(source, weight_ref[...].reshape(basis_count * channels, outs))
    own_ref[...] = total[:cells]
    pair_ref[...] = total[cells:].astype(pair_ref.dtype)


def backward_body(lay, offsets, own_ref, pair_ref, near_ref, next_ref, core_ref, cross_ref, taps_ref, index_ref,
                  weight_ref, own_grad_ref, pair_grad_ref, ext_scr, basis_scr, band_scr, sum_scr):
    rows, cols, _ = own_ref.shape
    basis_count, channels, outs = weight_ref.shape
    odd = lay.odd()
    place_rows(ext_scr, lambda v: v, own_ref, pair_ref, near_ref, next_ref, core_ref, cross_ref)
    weight = weight_ref[...].reshape(basis_count * channels, outs)
    first_row = (lax.axis_index("lat") - odd) * rows
    ext_rows, ext_cols, _ = ext_scr.shape
    blocks = ext_cols // TILE
    for row in range(ext_rows):
        basis_grad = dot(ext_scr[row], weight, NT).astype(bf16)
        low = row * basis_count * TILE
        for basis in range(basis_count):
            for block in range(blocks):
                piece = basis_grad[block * TILE : (block + 1) * TILE, basis * channels : (basis + 1) * channels]
                start = low + basis * TILE
                basis_scr[start : start + TILE, block * channels : (block + 1) * channels] = piece
        reached = [target + 2 * (offsets // 2) - row for target in range(2 * rows)]
        band_scr[low : low + basis_count * TILE, :] = bands(taps_ref, index_ref, first_row + row, basis_count, reached, offsets)
    sum_scr[...] = jnp.zeros(sum_scr.shape, f32)
    for block in range(0, blocks, 2):
        sides = min(2, blocks - block)
        spread = dot(band_scr[...], basis_scr[:, block * channels : (block + sides) * channels], TN)
        for target in range(2 * rows):
            for side in range(sides):
                start = (block + side) * TILE
                piece = spread[target * SLOT : (target + 1) * SLOT, side * channels : (side + 1) * channels]
                sum_scr[target, start : start + SLOT, :] = sum_scr[target, start : start + SLOT, :] + piece
    for row in range(rows):
        for ref, slot in ((own_grad_ref, odd * rows), (pair_grad_ref, (1 - odd) * rows)):
            ref[row * cols : (row + 1) * cols, :] = sum_scr[slot + row, TILE : TILE + cols, :].astype(bf16)


def finish_body(lay, own_ref, pair_ref, grad_ref):
    shape = (own_ref.shape[1], grad_ref.shape[1])
    place, column = lay.places(shape, 0), lax.broadcasted_iota(jnp.int32, shape, 1)
    odd = lay.odd()
    own = (column == lay.whole(place, odd)).astype(bf16)
    pair = (column == lay.whole(place, 1 - odd)).astype(bf16)
    grad_ref[...] = (dot(own_ref[...], own) + dot(pair_ref[...], pair)).astype(bf16)


def after(array, *others):
    return lax.optimization_barrier((array, *others))[0]


def swap(array, axis, stride):
    return lax.ppermute(array, axis, [(i, i ^ stride) for i in range(lax.axis_size(axis))])


def swap_across(array, axis, stride, wrap):
    size = lax.axis_size(axis)
    pairs = [(i, i + stride if i // stride % 2 else i - stride) for i in range(size)]
    return lax.ppermute(array, axis, [(i, j % size) for i, j in pairs if wrap or 0 <= j < size])


def flat(rows, width):
    wide = width // rows.shape[2]
    lines = [
        jnp.concatenate([rows[row + side] for side in range(wide)], axis=1) for row in range(0, rows.shape[0], wide)
    ]
    return jnp.concatenate(lines, axis=0)


def row_halo(own, pair, width, near_more):
    lat = lax.axis_index("lat")
    own_first = (lat & 1) != ((lat >> 1) & 1)
    to_near, to_far = jnp.where(own_first, own, pair), jnp.where(own_first, pair, own)
    near = swap(jnp.concatenate([flat(to_near, width), *near_more], axis=0), "lat", 2)
    return near, swap_across(flat(to_far, width), "lat", 2, False)


def edges(near, own, pair, far, rim, width):
    rows, cols, channels = own.shape
    lines = rows * channels // width

    def at(first):
        def halo(v):
            return [v[line * cols + first : line * cols + first + rim] for line in range(lines)]

        kept = [flat(v[:, first : first + rim], width) for v in (own, pair)]
        return jnp.concatenate([*halo(near), *kept, *halo(far)], axis=0)

    even = (lax.axis_index("lon") & 1) == 0
    left, right = at(0), at(cols - rim)
    return jnp.where(even, right, left), jnp.where(even, left, right)


def column_halo(lay, to_core, to_cross, cross_more):
    to_cross = jnp.concatenate([to_cross, *cross_more], axis=0)
    cross = swap(to_cross, "lon", 3) if lay.merged else swap_across(to_cross, "lon", 1, True)
    return swap(to_core, "lon", 1), cross


def local(features, weight, tap_values, basis_index, half_width, cotangent):
    channels, rows, cols = features.shape
    basis_count = weight.shape[0]
    _, offsets, window = tap_values.shape
    rim = (window - 1) // 2
    lay = Layout(channels, lax.axis_size("lat"), lax.axis_size("lon"))
    odd = lay.odd()
    half = channels // 2

    split = features.reshape(half // lay.pair, 2, lay.pair, rows, cols)
    to_pair = lax.dynamic_index_in_dim(split, 1 - odd, 1, False).reshape(half, rows, cols)
    to_keep = lax.dynamic_index_in_dim(split, odd, 1, False).reshape(half, rows, cols)
    feat_pair = jnp.transpose(swap(to_pair, "lat", 1), (1, 2, 0))
    feat_own = jnp.transpose(to_keep, (1, 2, 0))
    cot_pair = jnp.transpose(swap(cotangent, "lat", 1), (1, 2, 0))
    cot_own = jnp.transpose(cotangent, (1, 2, 0))

    far = jnp.abs(jnp.arange(window) - rim)
    index = jnp.where(far[None, None, :] <= half_width[:, None, None], basis_index, -1)
    fill = ((rows, rows), (0, offsets % 2), (0, SLOT - window))
    index = jnp.pad(index, fill, constant_values=-1)
    taps = jnp.pad(tap_values.astype(f32), fill)

    full = weight.reshape(basis_count, lay.own, channels // lay.parts)
    for axis, flip, _ in lay.split:
        other = swap(full, axis, flip)
        low = (lax.axis_index(axis) // flip) % 2 == 0
        full = jnp.where(low, jnp.concatenate([full, other], 2), jnp.concatenate([other, full], 2))
    gather = list(reversed(lay.steps))

    def widen(full, step):
        return jnp.concatenate([full, swap(full, step[0], step[1])], axis=1)

    lot = basis_count * lay.own

    def tail(array, count):
        return [array[array.shape[0] - (i + 1) * lot : array.shape[0] - i * lot] for i in reversed(range(count))]

    own, by_next = [], []
    if lay.merged:
        own = [after(weight, to_pair).reshape(lot, channels)]
        own = [lax.optimization_barrier(own[0])]
        by_next = [swap(own[0], "lat", 4)]
    near, far = row_halo(feat_own, feat_pair, channels, own)
    by_near = tail(near, len(own))
    to_core, to_cross = edges(near, feat_own, feat_pair, far, rim, channels)
    core, cross = column_halo(lay, to_core, to_cross, own + by_near)
    if not lay.merged:
        for step in gather[:-1]:
            full = widen(full, step)
    by_next = [after(v, to_core, to_cross) for v in by_next]
    cot_near, cot_far = row_halo(after(cot_own, to_core, to_cross), cot_pair, channels, by_next)

    cells = rows * cols
    ext = (4 * rows, cols + 2 * rim)
    basis_out, send, keep = call(
        lambda *refs: forward_body(lay, offsets, *refs), "forward", 16 * basis_count * cells * half * channels,
        [((basis_count, 2 * cells, half), bf16), ((basis_count, half // 2, channels), f32),
         ((basis_count, half // 2, channels), f32)],
        feat_own, feat_pair, near, far, core, cross, taps, index, cot_own, cot_pair,
        scratch=[pltpu.VMEM((*ext, half), bf16)],
    )
    for rank, (axis, flip, _) in enumerate(lay.steps):
        terms = (keep, swap(send, axis, flip))
        if rank == 0:
            cot_near, cot_far = after(cot_near, send), after(cot_far, send)
        elif rank == 1:
            by_both = tail(cot_near, len(own))
            to_core, to_cross = edges(cot_near, cot_own, cot_pair, cot_far, rim, channels)
            to_core, to_cross = after(to_core, send), after(to_cross, send)
            cot_core, cot_cross = column_halo(lay, to_core, to_cross, by_next + by_both)
        elif rank == 2:
            cot_core, cot_cross = after(cot_core, send), after(cot_cross, send)
            cot_around = (cot_near, cot_far, cot_core, cot_cross)
            if lay.merged:
                crossed, crossed_last = tail(cross, 2), tail(cot_cross, 2)
                held = own + by_next + crossed[:1] + crossed_last[:1] + by_near + by_both + crossed[1:] + crossed_last[1:]
                full = jnp.concatenate([v.reshape(basis_count, lay.own, channels) for v in held], axis=1)
            full = widen(full, gather[-1])
            own_out, pair_out = call(
                mix_body, "mix", 4 * basis_count * cells * half * channels, [((cells, channels), f32), ((cells, channels), bf16)], full, basis_out
            )
            cot_after = after(cot_own, pair_out)
            pair_out = swap(pair_out, "lat", 1)
            cot_around = (cot_near, cot_far, cot_core, cot_cross)
            own_grad, pair_grad = call(
                lambda *refs: backward_body(lay, offsets, *refs), "backward", 48 * basis_count * cells * half * channels,
                [((cells, half), bf16), ((cells, half), bf16)],
                cot_after, cot_pair, *cot_around, taps, index, full,
                scratch=[pltpu.VMEM((*ext, channels), bf16),
                         pltpu.VMEM((ext[0] * basis_count * TILE, ext[1] // TILE * half), bf16),
                         pltpu.VMEM((ext[0] * basis_count * TILE, 2 * rows * SLOT), bf16),
                         pltpu.VMEM((2 * rows, ext[1] + TILE, half), f32)],
            )
            pair_grad = swap(pair_grad, "lat", 1)
        if rank + 1 < len(lay.steps):
            size = keep.shape[1] // 2
            send = (terms[0][:, size:] + terms[1][:, size:]).astype(bf16 if rank < 2 else f32)
            keep = terms[0][:, :size] + terms[1][:, :size]
    grad = terms[0] + terms[1]
    for axis, flip, _ in reversed(lay.split):
        size = grad.shape[2] // 2
        odd_part = (lax.axis_index(axis) // flip) % 2
        other = swap(lax.dynamic_slice_in_dim(grad, (1 - odd_part) * size, size, 2), axis, flip)
        grad = lax.dynamic_slice_in_dim(grad, odd_part * size, size, 2) + other
    weight_grad = grad.reshape(basis_count, weight.shape[1])

    output = (own_out + pair_out).astype(bf16)
    (input_grad,) = call(
        lambda *refs: finish_body(lay, *refs), "finish", 4 * cells * half * channels, [((cells, channels), bf16)], own_grad, pair_grad
    )

    def channels_first(v):
        return jnp.transpose(v.reshape(rows, cols, channels), (2, 0, 1))

    return channels_first(output), channels_first(input_grad), weight_grad


def solution(mesh):
    field = P(None, "lat", "lon")
    flat = P(None, ("lat", "lon"))
    return jax.shard_map(
        local,
        mesh=mesh,
        in_specs=(field, flat, P(), P(), P(), field),
        out_specs=(field, field, flat),
        check_vma=False,
    )
```

```python
import jax
import jax.numpy as jnp
from jax import lax
from jax.experimental import pallas as pl
from jax.experimental.pallas import tpu as pltpu
from jax.sharding import PartitionSpec as P

TILE = 32
SLOT = 64
VMEM = 16 * 1024 * 1024
NT = (((1,), (1,)), ((), ()))
TN = (((0,), (0,)), ((), ()))
bf16, f32 = jnp.bfloat16, jnp.float32


def dot(a, b, dims=(((1,), (0,)), ((), ()))):
    return lax.dot_general(a, b, dims, preferred_element_type=f32)


def call(body, name, flops, outs, *args, scratch=()):
    in_vmem = pl.BlockSpec(memory_space=pltpu.VMEM)
    return pl.pallas_call(
        body,
        name=name,
        out_shape=[jax.ShapeDtypeStruct(s, d) for s, d in outs],
        in_specs=[in_vmem for _ in args],
        out_specs=[in_vmem for _ in outs],
        scratch_shapes=list(scratch),
        cost_estimate=pl.CostEstimate(
            flops=flops, transcendentals=0, bytes_accessed=sum(v.size * v.dtype.itemsize for v in args)
        ),
        compiler_params=pltpu.CompilerParams(vmem_limit_bytes=VMEM),
    )(*args)


def log2(size):
    return size.bit_length() - 1


class Layout:
    def __init__(self, channels, lats, lons):
        self.channels, self.lons = channels, lons
        devices = lats * lons
        self.parts = max(1, devices // channels)
        self.own = channels * self.parts // devices
        self.bits = [1 << b for b in range(devices.bit_length() - 1) if 1 << b != lons]
        self.merged = lats == 8 and lons == 4 and self.parts == 1
        if self.merged:
            steps = [("lon", 1), ("lat", 2), ("lon", 3), ("lat", 4)]
        else:
            steps = [("lon", 1 << b) for b in range(lons.bit_length() - 1)]
            steps += [("lat", 2 << b) for b in range(lats.bit_length() - 2)]
        steps = [(axis, flip, flip if axis == "lon" else flip * lons) for axis, flip in steps]
        self.split = [s for s in steps if s[2] < self.parts]
        self.steps = [s for s in steps if s[2] >= self.parts]
        self.pair = lons // self.parts * self.own

    def odd(self):
        return lax.axis_index("lat") & 1

    def places(self, shape, dim):
        place = lax.broadcasted_iota(jnp.int32, shape, dim)
        owner = lax.axis_index("lat") * self.lons + lax.axis_index("lon")
        for rank, (_, _, flip) in enumerate(self.steps):
            owner = owner ^ (((place >> log2(self.channels >> (rank + 2))) & 1) * flip)
        channel = place & (self.own - 1)
        for bit in self.bits:
            if bit >= self.parts:
                value = bit // self.parts * self.own
                value = value // 2 if value > self.pair else value
                channel = channel + (((owner >> log2(bit)) & 1) << log2(value))
        return channel

    def whole(self, channel, odd):
        low = log2(self.pair)
        return ((channel >> low) << (low + 1)) + (odd << low) + (channel & (self.pair - 1))


def bands(taps_ref, index_ref, row, basis_count, picked, offsets):
    taps, index = taps_ref[row], index_ref[row]

    def line(v, a, none):
        return v[a : a + 1] if 0 <= a < offsets else jnp.full((1, SLOT), none, v.dtype)

    def paired(v, none):
        return [
            jnp.concatenate([line(v, a, none), line(v, b, none)], axis=1)
            for a, b in zip(picked[::2], picked[1::2] + [-1] * (len(picked) % 2))
        ]

    taps, index = paired(taps, 0.0), paired(index, -1)
    parts = []
    for basis in range(basis_count):
        pieces = []
        for value, kind in zip(taps, index):
            piece = jnp.broadcast_to(jnp.where(kind == basis, value, 0.0), (TILE, 2 * SLOT))
            pieces.append(pltpu.roll(piece, 0, 1, stride=1, stride_axis=0))
        parts.append(jnp.concatenate(pieces, axis=1).astype(bf16))
    return jnp.concatenate(parts, axis=0)


def place_rows(scr, move, own_ref, pair_ref, near_ref, next_ref, core_ref, cross_ref, base, rim_base):
    rows, cols, _ = own_ref.shape
    channels = scr.shape[2]
    lat, lon = lax.axis_index("lat"), lax.axis_index("lon")
    odd, flip = lat & 1, (lat >> 1) & 1
    even_col = (lon & 1) == 0
    rim = (scr.shape[1] - cols) // 2
    wide = near_ref.shape[1] // channels

    def part(ref, first, row, length):
        low = first + row // wide * length
        return ref[low : low + length, row % wide * channels : (row % wide + 1) * channels]

    slots = ((1 - flip) * 3 * rows, (1 + odd) * rows, (2 - odd) * rows, flip * 3 * rows)
    for rank, slot in enumerate(slots):
        for row in range(rows):
            if rank in (0, 3):
                line = part((near_ref, next_ref)[rank // 3], base, row, cols)
            else:
                line = (own_ref, pair_ref)[rank - 1][row]
            first = rim_base + rank * (rows // wide) * rim
            core, cross = part(core_ref, first, row, rim), part(cross_ref, first, row, rim)
            scr[slot + row, rim : rim + cols, :] = move(line)
            scr[slot + row, :rim, :] = move(jnp.where(even_col, cross, core))
            scr[slot + row, rim + cols :, :] = move(jnp.where(even_col, core, cross))


def forward_body(lay, offsets, own_ref, pair_ref, near_ref, next_ref, core_ref, cross_ref, taps_ref, index_ref,
                 own_cot_ref, pair_cot_ref, out_ref, send_ref, keep_ref, ext_scr):
    rows, cols, _ = own_ref.shape
    basis_count, _, channels = out_ref.shape
    odd = lay.odd()
    shape = (channels, channels)
    pick = (lax.broadcasted_iota(jnp.int32, shape, 0) == lay.places(shape, 1)).astype(bf16)
    place_rows(
        ext_scr, lambda v: dot(v, pick).astype(bf16),
        own_ref, pair_ref, near_ref, next_ref, core_ref, cross_ref, 0, 0,
    )
    first_row = (lax.axis_index("lat") - odd) * rows
    for line in range(2 * rows):
        low = (odd if line < rows else 1 - odd) * rows + line % rows
        picked = list(range(offsets))
        band = bands(taps_ref, index_ref, first_row + low + rows, basis_count, picked, offsets)[:, : offsets * SLOT]
        for first in range(0, cols, 2 * TILE):
            source = [
                jnp.concatenate([ext_scr[low + a, start : start + SLOT, :] for a in range(offsets)], axis=0)
                for start in (first, first + TILE)
            ]
            moved = dot(band, jnp.concatenate(source, axis=1)).astype(bf16)
            for basis in range(basis_count):
                for side in range(2):
                    start = line * cols + first + side * TILE
                    piece = moved[basis * TILE : (basis + 1) * TILE, side * channels : (side + 1) * channels]
                    out_ref[basis, start : start + TILE, :] = piece
    cot = jnp.concatenate([own_cot_ref[...], pair_cot_ref[...]], axis=0).reshape(2 * rows * cols, own_cot_ref.shape[2])
    half = channels // 2
    for basis in range(basis_count):
        terms = dot(out_ref[basis], cot, TN)
        send_ref[basis] = terms[half:].astype(send_ref.dtype)
        keep_ref[basis] = terms[:half]


def mix_body(weight_ref, basis_ref, own_ref, pair_ref):
    basis_count, channels, outs = weight_ref.shape
    cells = own_ref.shape[0]
    source = jnp.concatenate([basis_ref[basis] for basis in range(basis_count)], axis=1)
    total = dot(source, weight_ref[...].reshape(basis_count * channels, outs))
    own_ref[...] = total[:cells]
    pair_ref[...] = total[cells:].astype(pair_ref.dtype)


def backward_body(lay, offsets, own_ref, pair_ref, near_ref, next_ref, core_ref, cross_ref, taps_ref, index_ref,
                  weight_ref, own_grad_ref, pair_grad_ref, ext_scr, basis_scr, band_scr, sum_scr):
    rows, cols, _ = own_ref.shape
    basis_count, channels, outs = weight_ref.shape
    odd = lay.odd()
    rim = (ext_scr.shape[1] - cols) // 2
    beside = outs // channels
    place_rows(
        ext_scr, lambda v: v, own_ref, pair_ref, near_ref, next_ref, core_ref, cross_ref,
        rows // beside * cols, 4 * (rows // beside) * rim,
    )
    weight = weight_ref[...].reshape(basis_count * channels, outs)
    first_row = (lax.axis_index("lat") - odd) * rows
    ext_rows, ext_cols, _ = ext_scr.shape
    blocks = ext_cols // TILE
    for row in range(ext_rows):
        basis_grad = dot(ext_scr[row], weight, NT).astype(bf16)
        low = row * basis_count * TILE
        for basis in range(basis_count):
            for block in range(blocks):
                piece = basis_grad[block * TILE : (block + 1) * TILE, basis * channels : (basis + 1) * channels]
                start = low + basis * TILE
                basis_scr[start : start + TILE, block * channels : (block + 1) * channels] = piece
        reached = [target + 2 * (offsets // 2) - row for target in range(2 * rows)]
        band_scr[low : low + basis_count * TILE, :] = bands(taps_ref, index_ref, first_row + row, basis_count, reached, offsets)
    sum_scr[...] = jnp.zeros(sum_scr.shape, f32)
    for block in range(0, blocks, 2):
        sides = min(2, blocks - block)
        spread = dot(band_scr[...], basis_scr[:, block * channels : (block + sides) * channels], TN)
        for target in range(2 * rows):
            for side in range(sides):
                start = (block + side) * TILE
                piece = spread[target * SLOT : (target + 1) * SLOT, side * channels : (side + 1) * channels]
                sum_scr[target, start : start + SLOT, :] = sum_scr[target, start : start + SLOT, :] + piece
    for row in range(rows):
        for ref, slot in ((own_grad_ref, odd * rows), (pair_grad_ref, (1 - odd) * rows)):
            ref[row * cols : (row + 1) * cols, :] = sum_scr[slot + row, TILE : TILE + cols, :].astype(bf16)


def finish_body(lay, own_ref, pair_ref, grad_ref):
    shape = (own_ref.shape[1], grad_ref.shape[1])
    place, column = lay.places(shape, 0), lax.broadcasted_iota(jnp.int32, shape, 1)
    odd = lay.odd()
    own = (column == lay.whole(place, odd)).astype(bf16)
    pair = (column == lay.whole(place, 1 - odd)).astype(bf16)
    grad_ref[...] = (dot(own_ref[...], own) + dot(pair_ref[...], pair)).astype(bf16)


def after(array, *others):
    return lax.optimization_barrier((array, *others))[0]


def swap(array, axis, stride):
    return lax.ppermute(array, axis, [(i, i ^ stride) for i in range(lax.axis_size(axis))])


def swap_across(array, axis, stride, wrap):
    size = lax.axis_size(axis)
    pairs = [(i, i + stride if i // stride % 2 else i - stride) for i in range(size)]
    return lax.ppermute(array, axis, [(i, j % size) for i, j in pairs if wrap or 0 <= j < size])


def flat(rows, width):
    wide = width // rows.shape[2]
    lines = [
        jnp.concatenate([rows[row + side] for side in range(wide)], axis=1) for row in range(0, rows.shape[0], wide)
    ]
    return jnp.concatenate(lines, axis=0)


def row_halo(own, pair, near_more):
    lat = lax.axis_index("lat")
    own_first = (lat & 1) != ((lat >> 1) & 1)
    width = own[1].shape[2]
    to_near = [flat(jnp.where(own_first, a, b), width) for a, b in zip(own, pair)]
    to_far = [flat(jnp.where(own_first, b, a), width) for a, b in zip(own, pair)]
    near = swap(jnp.concatenate([*to_near, *near_more], axis=0), "lat", 2)
    return near, swap_across(jnp.concatenate(to_far, axis=0), "lat", 2, False)


def edges(near, own, pair, far, rim):
    rows, cols, width = own[1].shape

    def at(first):
        fields, base = [], 0
        for a, b in zip(own, pair):
            lines = rows * a.shape[2] // width
            starts = [base + line * cols + first for line in range(lines)]
            kept = [flat(v[:, first : first + rim], width) for v in (a, b)]
            fields += [near[start : start + rim] for start in starts] + kept + [far[start : start + rim] for start in starts]
            base += lines * cols
        return jnp.concatenate(fields, axis=0)

    even = (lax.axis_index("lon") & 1) == 0
    left, right = at(0), at(cols - rim)
    return jnp.where(even, right, left), jnp.where(even, left, right)


def column_halo(lay, to_core, to_cross):
    cross = swap(to_cross, "lon", 3) if lay.merged else swap_across(to_cross, "lon", 1, True)
    return swap(to_core, "lon", 1), cross


def local(features, weight, tap_values, basis_index, half_width, cotangent):
    channels, rows, cols = features.shape
    basis_count = weight.shape[0]
    _, offsets, window = tap_values.shape
    rim = (window - 1) // 2
    lay = Layout(channels, lax.axis_size("lat"), lax.axis_size("lon"))
    odd = lay.odd()
    half = channels // 2

    split = features.reshape(half // lay.pair, 2, lay.pair, rows, cols)
    to_pair = lax.dynamic_index_in_dim(split, 1 - odd, 1, False).reshape(half, rows, cols)
    to_keep = lax.dynamic_index_in_dim(split, odd, 1, False).reshape(half, rows, cols)
    def channels_last(v):
        return jnp.transpose(v, (1, 2, 0))

    pair = channels_last(swap(to_pair, "lat", 1)), channels_last(swap(cotangent, "lat", 1))
    mine = channels_last(to_keep), channels_last(cotangent)

    far = jnp.abs(jnp.arange(window) - rim)
    index = jnp.where(far[None, None, :] <= half_width[:, None, None], basis_index, -1)
    fill = ((rows, rows), (0, offsets % 2), (0, SLOT - window))
    index = jnp.pad(index, fill, constant_values=-1)
    taps = jnp.pad(tap_values.astype(f32), fill)

    full = weight.reshape(basis_count, lay.own, channels // lay.parts)
    for axis, flip, _ in lay.split:
        other = swap(full, axis, flip)
        low = (lax.axis_index(axis) // flip) % 2 == 0
        full = jnp.where(low, jnp.concatenate([full, other], 2), jnp.concatenate([other, full], 2))
    gather = list(reversed(lay.steps))

    def widen(full, step):
        return jnp.concatenate([full, swap(full, step[0], step[1])], axis=1)

    lot = basis_count * lay.own

    def tail(array, count):
        return [array[array.shape[0] - (i + 1) * lot : array.shape[0] - i * lot] for i in reversed(range(count))]

    own = [lax.optimization_barrier(weight.reshape(lot, channels))] if lay.merged else []
    near, far = row_halo(mine, pair, own)
    by_near = tail(near, len(own))
    to_core, to_cross = edges(near, mine, pair, far, rim)
    core, cross = column_halo(lay, to_core, to_cross)
    if lay.merged:
        held = jnp.concatenate(own + by_near, axis=0)
        held = [held, swap(after(held, to_core, to_cross), "lat", 4)]
    else:
        for step in gather[:-1]:
            full = widen(full, step)

    cells = rows * cols
    ext = (4 * rows, cols + 2 * rim)
    basis_out, send, keep = call(
        lambda *refs: forward_body(lay, offsets, *refs), "forward", 16 * basis_count * cells * half * channels,
        [((basis_count, 2 * cells, half), bf16), ((basis_count, half // 2, channels), f32),
         ((basis_count, half // 2, channels), f32)],
        mine[0], pair[0], near, far, core, cross, taps, index, mine[1], pair[1],
        scratch=[pltpu.VMEM((*ext, half), bf16)],
    )
    for rank, (axis, flip, _) in enumerate(lay.steps):
        terms = (keep, swap(send, axis, flip))
        if rank == 2:
            terms = (keep, after(terms[1], own_grad))
        elif rank == 0:
            if lay.merged:
                held = [after(v, send) for v in held]
                (first, third), (second, fourth) = ((v[:lot], v[lot:]) for v in held)
                held = jnp.concatenate([first, second, third, fourth], axis=0)
                other = swap(held, "lon", 3)
        elif rank == 1:
            if lay.merged:
                other = after(other, send)
                blocks = [v[i * lot : (i + 1) * lot] for v, i in ((held, 0), (held, 1), (other, 0), (other, 1),
                                                                  (held, 2), (held, 3), (other, 2), (other, 3))]
                full = jnp.concatenate([v.reshape(basis_count, lay.own, channels) for v in blocks], axis=1)
            full = widen(full, gather[-1])
            own_out, pair_out = call(
                mix_body, "mix", 4 * basis_count * cells * half * channels, [((cells, channels), f32), ((cells, channels), bf16)], full, basis_out
            )
            mine_after = after(mine[1], pair_out)
            pair_out = swap(pair_out, "lat", 1)
            own_grad, pair_grad = call(
                lambda *refs: backward_body(lay, offsets, *refs), "backward", 48 * basis_count * cells * half * channels,
                [((cells, half), bf16), ((cells, half), bf16)],
                mine_after, pair[1], near, far, core, cross, taps, index, full,
                scratch=[pltpu.VMEM((*ext, channels), bf16),
                         pltpu.VMEM((ext[0] * basis_count * TILE, ext[1] // TILE * half), bf16),
                         pltpu.VMEM((ext[0] * basis_count * TILE, 2 * rows * SLOT), bf16),
                         pltpu.VMEM((2 * rows, ext[1] + TILE, half), f32)],
            )
            pair_grad = swap(pair_grad, "lat", 1)
        if rank + 1 < len(lay.steps):
            size = keep.shape[1] // 2
            send = (terms[0][:, size:] + terms[1][:, size:]).astype(bf16 if rank < 3 else f32)
            keep = terms[0][:, :size] + terms[1][:, :size]
    output = (own_out + pair_out).astype(bf16)
    (input_grad,) = call(
        lambda *refs: finish_body(lay, *refs), "finish", 4 * cells * half * channels, [((cells, channels), bf16)], own_grad, pair_grad
    )

    def channels_first(v):
        return jnp.transpose(v.reshape(rows, cols, channels), (2, 0, 1))

    output, input_grad = channels_first(output), channels_first(input_grad)
    grad = terms[0] + after(terms[1], output, input_grad)
    for axis, flip, _ in reversed(lay.split):
        size = grad.shape[2] // 2
        odd_part = (lax.axis_index(axis) // flip) % 2
        other = swap(lax.dynamic_slice_in_dim(grad, (1 - odd_part) * size, size, 2), axis, flip)
        grad = lax.dynamic_slice_in_dim(grad, odd_part * size, size, 2) + other
    weight_grad = grad.reshape(basis_count, weight.shape[1])

    return output, input_grad, weight_grad


def solution(mesh):
    field = P(None, "lat", "lon")
    flat = P(None, ("lat", "lon"))
    return jax.shard_map(
        local,
        mesh=mesh,
        in_specs=(field, flat, P(), P(), P(), field),
        out_specs=(field, field, flat),
        check_vma=False,
    )
```

```python
import jax
import jax.numpy as jnp
from jax import lax
from jax.experimental import pallas as pl
from jax.experimental.pallas import tpu as pltpu
from jax.sharding import PartitionSpec as P

TILE = 32
SLOT = 64
VMEM = 16 * 1024 * 1024
NT = (((1,), (1,)), ((), ()))
TN = (((0,), (0,)), ((), ()))
bf16, f32 = jnp.bfloat16, jnp.float32


def dot(a, b, dims=(((1,), (0,)), ((), ()))):
    return lax.dot_general(a, b, dims, preferred_element_type=f32)


def call(body, name, flops, outs, *args, scratch=()):
    in_vmem = pl.BlockSpec(memory_space=pltpu.VMEM)
    return pl.pallas_call(
        body,
        name=name,
        out_shape=[jax.ShapeDtypeStruct(s, d) for s, d in outs],
        in_specs=[in_vmem for _ in args],
        out_specs=[in_vmem for _ in outs],
        scratch_shapes=list(scratch),
        cost_estimate=pl.CostEstimate(
            flops=flops, transcendentals=0, bytes_accessed=sum(v.size * v.dtype.itemsize for v in args)
        ),
        compiler_params=pltpu.CompilerParams(vmem_limit_bytes=VMEM),
    )(*args)


def log2(size):
    return size.bit_length() - 1


class Layout:
    def __init__(self, channels, lats, lons):
        self.channels, self.lons = channels, lons
        devices = lats * lons
        self.parts = max(1, devices // channels)
        self.own = channels * self.parts // devices
        self.bits = [1 << b for b in range(devices.bit_length() - 1) if 1 << b != lons]
        self.merged = lats == 8 and lons == 4 and self.parts == 1
        if self.merged:
            steps = [("lon", 1), ("lat", 2), ("lon", 3), ("lat", 4)]
        else:
            steps = [("lon", 1 << b) for b in range(lons.bit_length() - 1)]
            steps += [("lat", 2 << b) for b in range(lats.bit_length() - 2)]
        steps = [(axis, flip, flip if axis == "lon" else flip * lons) for axis, flip in steps]
        self.split = [s for s in steps if s[2] < self.parts]
        self.steps = [s for s in steps if s[2] >= self.parts]
        self.pair = lons // self.parts * self.own

    def odd(self):
        return lax.axis_index("lat") & 1

    def places(self, shape, dim):
        place = lax.broadcasted_iota(jnp.int32, shape, dim)
        owner = lax.axis_index("lat") * self.lons + lax.axis_index("lon")
        for rank, (_, _, flip) in enumerate(self.steps):
            owner = owner ^ (((place >> log2(self.channels >> (rank + 2))) & 1) * flip)
        channel = place & (self.own - 1)
        for bit in self.bits:
            if bit >= self.parts:
                value = bit // self.parts * self.own
                value = value // 2 if value > self.pair else value
                channel = channel + (((owner >> log2(bit)) & 1) << log2(value))
        return channel

    def whole(self, channel, odd):
        low = log2(self.pair)
        return ((channel >> low) << (low + 1)) + (odd << low) + (channel & (self.pair - 1))


def bands(taps_ref, index_ref, row, basis_count, picked, offsets):
    taps, index = taps_ref[row], index_ref[row]

    def line(v, a, none):
        return v[a : a + 1] if 0 <= a < offsets else jnp.full((1, SLOT), none, v.dtype)

    def paired(v, none):
        return [
            jnp.concatenate([line(v, a, none), line(v, b, none)], axis=1)
            for a, b in zip(picked[::2], picked[1::2] + [-1] * (len(picked) % 2))
        ]

    taps, index = paired(taps, 0.0), paired(index, -1)
    parts = []
    for basis in range(basis_count):
        pieces = []
        for value, kind in zip(taps, index):
            piece = jnp.broadcast_to(jnp.where(kind == basis, value, 0.0), (TILE, 2 * SLOT))
            pieces.append(pltpu.roll(piece, 0, 1, stride=1, stride_axis=0))
        parts.append(jnp.concatenate(pieces, axis=1).astype(bf16))
    return jnp.concatenate(parts, axis=0)


def place_rows(scr, move, own_ref, pair_ref, near_ref, next_ref, core_ref, cross_ref, base, rim_base):
    rows, cols, _ = own_ref.shape
    channels = scr.shape[2]
    lat, lon = lax.axis_index("lat"), lax.axis_index("lon")
    odd, flip = lat & 1, (lat >> 1) & 1
    even_col = (lon & 1) == 0
    rim = (scr.shape[1] - cols) // 2
    wide = near_ref.shape[1] // channels

    def part(ref, first, row, length):
        low = first + row // wide * length
        return ref[low : low + length, row % wide * channels : (row % wide + 1) * channels]

    slots = ((1 - flip) * 3 * rows, (1 + odd) * rows, (2 - odd) * rows, flip * 3 * rows)
    for rank, slot in enumerate(slots):
        for row in range(rows):
            if rank in (0, 3):
                line = part((near_ref, next_ref)[rank // 3], base, row, cols)
            else:
                line = (own_ref, pair_ref)[rank - 1][row]
            first = rim_base + rank * (rows // wide) * rim
            core, cross = part(core_ref, first, row, rim), part(cross_ref, first, row, rim)
            scr[slot + row, rim : rim + cols, :] = move(line)
            scr[slot + row, :rim, :] = move(jnp.where(even_col, cross, core))
            scr[slot + row, rim + cols :, :] = move(jnp.where(even_col, core, cross))


def forward_body(lay, offsets, own_ref, pair_ref, near_ref, next_ref, core_ref, cross_ref, taps_ref, index_ref,
                 own_cot_ref, pair_cot_ref, out_ref, send_ref, keep_ref, ext_scr):
    rows, cols, _ = own_ref.shape
    basis_count, _, channels = out_ref.shape
    odd = lay.odd()
    shape = (channels, channels)
    pick = (lax.broadcasted_iota(jnp.int32, shape, 0) == lay.places(shape, 1)).astype(bf16)
    place_rows(
        ext_scr, lambda v: dot(v, pick).astype(bf16),
        own_ref, pair_ref, near_ref, next_ref, core_ref, cross_ref, 0, 0,
    )
    first_row = (lax.axis_index("lat") - odd) * rows
    for line in range(2 * rows):
        low = (odd if line < rows else 1 - odd) * rows + line % rows
        picked = list(range(offsets))
        band = bands(taps_ref, index_ref, first_row + low + rows, basis_count, picked, offsets)[:, : offsets * SLOT]
        for first in range(0, cols, 2 * TILE):
            source = [
                jnp.concatenate([ext_scr[low + a, start : start + SLOT, :] for a in range(offsets)], axis=0)
                for start in (first, first + TILE)
            ]
            moved = dot(band, jnp.concatenate(source, axis=1)).astype(bf16)
            for basis in range(basis_count):
                for side in range(2):
                    start = line * cols + first + side * TILE
                    piece = moved[basis * TILE : (basis + 1) * TILE, side * channels : (side + 1) * channels]
                    out_ref[basis, start : start + TILE, :] = piece
    cot = jnp.concatenate([own_cot_ref[...], pair_cot_ref[...]], axis=0).reshape(2 * rows * cols, own_cot_ref.shape[2])
    half = channels // 2
    for basis in range(basis_count):
        terms = dot(out_ref[basis], cot, TN)
        send_ref[basis] = terms[half:].astype(send_ref.dtype)
        keep_ref[basis] = terms[:half]


def mix_body(weight_ref, basis_ref, own_ref, pair_ref):
    basis_count, channels, outs = weight_ref.shape
    cells = own_ref.shape[0]
    source = jnp.concatenate([basis_ref[basis] for basis in range(basis_count)], axis=1)
    total = dot(source, weight_ref[...].reshape(basis_count * channels, outs))
    own_ref[...] = total[:cells]
    pair_ref[...] = total[cells:].astype(pair_ref.dtype)


def backward_body(lay, offsets, own_ref, pair_ref, near_ref, next_ref, core_ref, cross_ref, taps_ref, index_ref,
                  weight_ref, own_grad_ref, pair_grad_ref, ext_scr, basis_scr, band_scr, sum_scr):
    rows, cols, _ = own_ref.shape
    basis_count, channels, outs = weight_ref.shape
    odd = lay.odd()
    rim = (ext_scr.shape[1] - cols) // 2
    beside = outs // channels
    place_rows(
        ext_scr, lambda v: v, own_ref, pair_ref, near_ref, next_ref, core_ref, cross_ref,
        rows // beside * cols, 4 * (rows // beside) * rim,
    )
    weight = weight_ref[...].reshape(basis_count * channels, outs)
    first_row = (lax.axis_index("lat") - odd) * rows
    ext_rows, ext_cols, _ = ext_scr.shape
    blocks = ext_cols // TILE
    for row in range(ext_rows):
        basis_grad = dot(ext_scr[row], weight, NT).astype(bf16)
        low = row * basis_count * TILE
        for basis in range(basis_count):
            for block in range(blocks):
                piece = basis_grad[block * TILE : (block + 1) * TILE, basis * channels : (basis + 1) * channels]
                start = low + basis * TILE
                basis_scr[start : start + TILE, block * channels : (block + 1) * channels] = piece
        reached = [target + 2 * (offsets // 2) - row for target in range(2 * rows)]
        band_scr[low : low + basis_count * TILE, :] = bands(taps_ref, index_ref, first_row + row, basis_count, reached, offsets)
    sum_scr[...] = jnp.zeros(sum_scr.shape, f32)
    for block in range(0, blocks, 2):
        sides = min(2, blocks - block)
        spread = dot(band_scr[...], basis_scr[:, block * channels : (block + sides) * channels], TN)
        for target in range(2 * rows):
            for side in range(sides):
                start = (block + side) * TILE
                piece = spread[target * SLOT : (target + 1) * SLOT, side * channels : (side + 1) * channels]
                sum_scr[target, start : start + SLOT, :] = sum_scr[target, start : start + SLOT, :] + piece
    for row in range(rows):
        for ref, slot in ((own_grad_ref, odd * rows), (pair_grad_ref, (1 - odd) * rows)):
            ref[row * cols : (row + 1) * cols, :] = sum_scr[slot + row, TILE : TILE + cols, :].astype(bf16)


def finish_body(lay, own_ref, pair_ref, grad_ref):
    shape = (own_ref.shape[1], grad_ref.shape[1])
    place, column = lay.places(shape, 0), lax.broadcasted_iota(jnp.int32, shape, 1)
    odd = lay.odd()
    own = (column == lay.whole(place, odd)).astype(bf16)
    pair = (column == lay.whole(place, 1 - odd)).astype(bf16)
    grad_ref[...] = (dot(own_ref[...], own) + dot(pair_ref[...], pair)).astype(bf16)


def after(array, *others):
    return lax.optimization_barrier((array, *others))[0]


def swap(array, axis, stride):
    return lax.ppermute(array, axis, [(i, i ^ stride) for i in range(lax.axis_size(axis))])


def swap_across(array, axis, stride, wrap):
    size = lax.axis_size(axis)
    pairs = [(i, i + stride if i // stride % 2 else i - stride) for i in range(size)]
    return lax.ppermute(array, axis, [(i, j % size) for i, j in pairs if wrap or 0 <= j < size])


def flat(rows, width):
    wide = width // rows.shape[2]
    lines = [
        jnp.concatenate([rows[row + side] for side in range(wide)], axis=1) for row in range(0, rows.shape[0], wide)
    ]
    return jnp.concatenate(lines, axis=0)


def row_halo(own, pair, near_more):
    lat = lax.axis_index("lat")
    own_first = (lat & 1) != ((lat >> 1) & 1)
    width = own[1].shape[2]
    to_near = [flat(jnp.where(own_first, a, b), width) for a, b in zip(own, pair)]
    to_far = [flat(jnp.where(own_first, b, a), width) for a, b in zip(own, pair)]
    near = swap(jnp.concatenate([*to_near, *near_more], axis=0), "lat", 2)
    return near, swap_across(jnp.concatenate(to_far, axis=0), "lat", 2, False)


def edges(near, own, pair, far, rim):
    rows, cols, width = own[1].shape

    def at(first):
        fields, base = [], 0
        for a, b in zip(own, pair):
            lines = rows * a.shape[2] // width
            starts = [base + line * cols + first for line in range(lines)]
            kept = [flat(v[:, first : first + rim], width) for v in (a, b)]
            fields += [near[start : start + rim] for start in starts] + kept + [far[start : start + rim] for start in starts]
            base += lines * cols
        return jnp.concatenate(fields, axis=0)

    even = (lax.axis_index("lon") & 1) == 0
    left, right = at(0), at(cols - rim)
    return jnp.where(even, right, left), jnp.where(even, left, right)


def column_halo(lay, to_core, to_cross):
    cross = swap(to_cross, "lon", 3) if lay.merged else swap_across(to_cross, "lon", 1, True)
    return swap(to_core, "lon", 1), cross


def local(features, weight, tap_values, basis_index, half_width, cotangent):
    channels, rows, cols = features.shape
    basis_count = weight.shape[0]
    _, offsets, window = tap_values.shape
    rim = (window - 1) // 2
    lay = Layout(channels, lax.axis_size("lat"), lax.axis_size("lon"))
    odd = lay.odd()
    half = channels // 2

    split = features.reshape(half // lay.pair, 2, lay.pair * rows, cols)
    to_pair = lax.dynamic_index_in_dim(split, 1 - odd, 1, False).reshape(half * rows, cols)
    to_keep = lax.dynamic_index_in_dim(split, odd, 1, False).reshape(half, rows, cols)

    def channels_last(v):
        return jnp.transpose(v, (1, 2, 0))

    def from_pair(v):
        return channels_last(swap(v.reshape(-1, cols), "lat", 1).reshape(-1, rows, cols))

    pair_cot = from_pair(cotangent)
    pair = from_pair(to_pair), pair_cot
    mine = channels_last(to_keep), channels_last(cotangent)

    far = jnp.abs(jnp.arange(window) - rim)
    index = jnp.where(far[None, None, :] <= half_width[:, None, None], basis_index, -1)
    fill = ((rows, rows), (0, offsets % 2), (0, SLOT - window))
    index = jnp.pad(index, fill, constant_values=-1)
    taps = jnp.pad(tap_values.astype(f32), fill)

    full = weight.reshape(basis_count, lay.own, channels // lay.parts)
    for axis, flip, _ in lay.split:
        other = swap(full, axis, flip)
        low = (lax.axis_index(axis) // flip) % 2 == 0
        full = jnp.where(low, jnp.concatenate([full, other], 2), jnp.concatenate([other, full], 2))
    gather = list(reversed(lay.steps))

    def widen(full, step):
        return jnp.concatenate([full, swap(full, step[0], step[1])], axis=1)

    lot = basis_count * lay.own

    def tail(array, count):
        return [array[array.shape[0] - (i + 1) * lot : array.shape[0] - i * lot] for i in reversed(range(count))]

    own = [lax.optimization_barrier(weight.reshape(lot, channels))] if lay.merged else []
    near, far = row_halo(mine, pair, own)
    by_near = tail(near, len(own))
    to_core, to_cross = edges(near, mine, pair, far, rim)
    core, cross = column_halo(lay, to_core, to_cross)
    if lay.merged:
        held = jnp.concatenate(own + by_near, axis=0)
        held = [held, swap(after(held, to_core, to_cross), "lat", 4)]
    else:
        for step in gather[:-1]:
            full = widen(full, step)

    cells = rows * cols
    ext = (4 * rows, cols + 2 * rim)
    basis_out, send, keep = call(
        lambda *refs: forward_body(lay, offsets, *refs), "forward", 16 * basis_count * cells * half * channels,
        [((basis_count, 2 * cells, half), bf16), ((basis_count, half // 2, channels), f32),
         ((basis_count, half // 2, channels), f32)],
        mine[0], pair[0], near, far, core, cross, taps, index, mine[1], pair[1],
        scratch=[pltpu.VMEM((*ext, half), bf16)],
    )
    for rank, (axis, flip, _) in enumerate(lay.steps):
        terms = (keep, swap(send, axis, flip))
        if rank == 2:
            terms = (keep, after(terms[1], own_grad))
        elif rank == 0:
            if lay.merged:
                held = [after(v, send) for v in held]
                (first, third), (second, fourth) = ((v[:lot], v[lot:]) for v in held)
                held = jnp.concatenate([first, second, third, fourth], axis=0)
                other = swap(held, "lon", 3)
        elif rank == 1:
            if lay.merged:
                other = after(other, send)
                blocks = [v[i * lot : (i + 1) * lot] for v, i in ((held, 0), (held, 1), (other, 0), (other, 1),
                                                                  (held, 2), (held, 3), (other, 2), (other, 3))]
                full = jnp.concatenate([v.reshape(basis_count, lay.own, channels) for v in blocks], axis=1)
            full = widen(full, gather[-1])
            own_out, pair_out = call(
                mix_body, "mix", 4 * basis_count * cells * half * channels, [((cells, channels), f32), ((cells, channels), bf16)], full, basis_out
            )
            mine_after = after(mine[1], pair_out)
            pair_out = swap(pair_out, "lat", 1)
            own_grad, pair_grad = call(
                lambda *refs: backward_body(lay, offsets, *refs), "backward", 48 * basis_count * cells * half * channels,
                [((cells, half), bf16), ((cells, half), bf16)],
                mine_after, pair[1], near, far, core, cross, taps, index, full,
                scratch=[pltpu.VMEM((*ext, channels), bf16),
                         pltpu.VMEM((ext[0] * basis_count * TILE, ext[1] // TILE * half), bf16),
                         pltpu.VMEM((ext[0] * basis_count * TILE, 2 * rows * SLOT), bf16),
                         pltpu.VMEM((2 * rows, ext[1] + TILE, half), f32)],
            )
            pair_grad = swap(pair_grad, "lat", 1)
        if rank + 1 < len(lay.steps):
            size = keep.shape[1] // 2
            send = (terms[0][:, size:] + terms[1][:, size:]).astype(bf16 if rank < 3 else f32)
            keep = terms[0][:, :size] + terms[1][:, :size]
    output = (own_out + pair_out).astype(bf16)
    (input_grad,) = call(
        lambda *refs: finish_body(lay, *refs), "finish", 4 * cells * half * channels, [((cells, channels), bf16)], own_grad, pair_grad
    )

    def channels_first(v):
        return jnp.transpose(v.reshape(rows, cols, channels), (2, 0, 1))

    output, input_grad = channels_first(output), channels_first(input_grad)
    grad = terms[0] + after(terms[1], output, input_grad)
    for axis, flip, _ in reversed(lay.split):
        size = grad.shape[2] // 2
        odd_part = (lax.axis_index(axis) // flip) % 2
        other = swap(lax.dynamic_slice_in_dim(grad, (1 - odd_part) * size, size, 2), axis, flip)
        grad = lax.dynamic_slice_in_dim(grad, odd_part * size, size, 2) + other
    weight_grad = grad.reshape(basis_count, weight.shape[1])

    return output, input_grad, weight_grad


def solution(mesh):
    field = P(None, "lat", "lon")
    flat = P(None, ("lat", "lon"))
    return jax.shard_map(
        local,
        mesh=mesh,
        in_specs=(field, flat, P(), P(), P(), field),
        out_specs=(field, field, flat),
        check_vma=False,
    )
```

```python
import jax
import jax.numpy as jnp
from jax import lax
from jax.experimental import pallas as pl
from jax.experimental.pallas import tpu as pltpu
from jax.sharding import PartitionSpec as P

TILE = 32
SLOT = 64
VMEM = 16 * 1024 * 1024
NT = (((1,), (1,)), ((), ()))
TN = (((0,), (0,)), ((), ()))
bf16, f32 = jnp.bfloat16, jnp.float32


def dot(a, b, dims=(((1,), (0,)), ((), ()))):
    return lax.dot_general(a, b, dims, preferred_element_type=f32)


def call(body, name, outs, *args, scratch=()):
    in_vmem = pl.BlockSpec(memory_space=pltpu.VMEM)
    return pl.pallas_call(
        body,
        name=name,
        out_shape=[jax.ShapeDtypeStruct(s, d) for s, d in outs],
        in_specs=[in_vmem for _ in args],
        out_specs=[in_vmem for _ in outs],
        scratch_shapes=list(scratch),
        compiler_params=pltpu.CompilerParams(vmem_limit_bytes=VMEM),
    )(*args)


def log2(size):
    return size.bit_length() - 1


class Layout:
    def __init__(self, channels, lats, lons):
        self.channels, self.lons = channels, lons
        devices = lats * lons
        self.parts = max(1, devices // channels)
        self.own = channels * self.parts // devices
        self.bits = [1 << b for b in range(devices.bit_length() - 1) if 1 << b != lons]
        self.merged = lats == 8 and lons == 4 and self.parts == 1
        if self.merged:
            steps = [("lon", 1), ("lat", 2), ("lon", 3), ("lat", 4)]
        else:
            steps = [("lon", 1 << b) for b in range(lons.bit_length() - 1)]
            steps += [("lat", 2 << b) for b in range(lats.bit_length() - 2)]
        steps = [(axis, flip, flip if axis == "lon" else flip * lons) for axis, flip in steps]
        self.split = [s for s in steps if s[2] < self.parts]
        self.steps = [s for s in steps if s[2] >= self.parts]
        self.pair = lons // self.parts * self.own

    def odd(self):
        return lax.axis_index("lat") & 1

    def places(self, shape, dim):
        place = lax.broadcasted_iota(jnp.int32, shape, dim)
        owner = lax.axis_index("lat") * self.lons + lax.axis_index("lon")
        for rank, (_, _, flip) in enumerate(self.steps):
            owner = owner ^ (((place >> log2(self.channels >> (rank + 2))) & 1) * flip)
        channel = place & (self.own - 1)
        for bit in self.bits:
            if bit >= self.parts:
                value = bit // self.parts * self.own
                value = value // 2 if value > self.pair else value
                channel = channel + (((owner >> log2(bit)) & 1) << log2(value))
        return channel

    def whole(self, channel, odd):
        low = log2(self.pair)
        return ((channel >> low) << (low + 1)) + (odd << low) + (channel & (self.pair - 1))


def bands(taps_ref, index_ref, row, basis_count, picked, offsets):
    taps, index = taps_ref[row], index_ref[row]

    def line(v, a, none):
        return v[a : a + 1] if 0 <= a < offsets else jnp.full((1, SLOT), none, v.dtype)

    def paired(v, none):
        return [
            jnp.concatenate([line(v, a, none), line(v, b, none)], axis=1)
            for a, b in zip(picked[::2], picked[1::2] + [-1] * (len(picked) % 2))
        ]

    taps, index = paired(taps, 0.0), paired(index, -1)
    parts = []
    for basis in range(basis_count):
        pieces = []
        for value, kind in zip(taps, index):
            piece = jnp.broadcast_to(jnp.where(kind == basis, value, 0.0), (TILE, 2 * SLOT))
            pieces.append(pltpu.roll(piece, 0, 1, stride=1, stride_axis=0))
        parts.append(jnp.concatenate(pieces, axis=1).astype(bf16))
    return jnp.concatenate(parts, axis=0)


def place_rows(scr, move, own_ref, pair_ref, near_ref, next_ref, core_ref, cross_ref, base, rim_base):
    rows, cols, _ = own_ref.shape
    channels = scr.shape[2]
    lat, lon = lax.axis_index("lat"), lax.axis_index("lon")
    odd, flip = lat & 1, (lat >> 1) & 1
    even_col = (lon & 1) == 0
    rim = (scr.shape[1] - cols) // 2
    wide = near_ref.shape[1] // channels

    def part(ref, first, row, length):
        low = first + row // wide * length
        return ref[low : low + length, row % wide * channels : (row % wide + 1) * channels]

    slots = ((1 - flip) * 3 * rows, (1 + odd) * rows, (2 - odd) * rows, flip * 3 * rows)
    for rank, slot in enumerate(slots):
        for row in range(rows):
            if rank in (0, 3):
                line = part((near_ref, next_ref)[rank // 3], base, row, cols)
            else:
                line = (own_ref, pair_ref)[rank - 1][row]
            first = rim_base + rank * (rows // wide) * rim
            core, cross = part(core_ref, first, row, rim), part(cross_ref, first, row, rim)
            scr[slot + row, rim : rim + cols, :] = move(line)
            scr[slot + row, :rim, :] = move(jnp.where(even_col, cross, core))
            scr[slot + row, rim + cols :, :] = move(jnp.where(even_col, core, cross))


def forward_body(lay, offsets, own_ref, pair_ref, near_ref, next_ref, core_ref, cross_ref, taps_ref, index_ref,
                 own_cot_ref, pair_cot_ref, out_ref, send_ref, keep_ref, ext_scr):
    rows, cols, _ = own_ref.shape
    basis_count, _, channels = out_ref.shape
    odd = lay.odd()
    shape = (channels, channels)
    pick = (lax.broadcasted_iota(jnp.int32, shape, 0) == lay.places(shape, 1)).astype(bf16)
    place_rows(
        ext_scr, lambda v: dot(v, pick).astype(bf16),
        own_ref, pair_ref, near_ref, next_ref, core_ref, cross_ref, 0, 0,
    )
    first_row = (lax.axis_index("lat") - odd) * rows
    for line in range(2 * rows):
        low = (odd if line < rows else 1 - odd) * rows + line % rows
        picked = list(range(offsets))
        band = bands(taps_ref, index_ref, first_row + low + rows, basis_count, picked, offsets)[:, : offsets * SLOT]
        for first in range(0, cols, 2 * TILE):
            source = [
                jnp.concatenate([ext_scr[low + a, start : start + SLOT, :] for a in range(offsets)], axis=0)
                for start in (first, first + TILE)
            ]
            moved = dot(band, jnp.concatenate(source, axis=1)).astype(bf16)
            for basis in range(basis_count):
                for side in range(2):
                    start = line * cols + first + side * TILE
                    piece = moved[basis * TILE : (basis + 1) * TILE, side * channels : (side + 1) * channels]
                    out_ref[basis, start : start + TILE, :] = piece
    cot = jnp.concatenate([own_cot_ref[...], pair_cot_ref[...]], axis=0).reshape(2 * rows * cols, own_cot_ref.shape[2])
    half = channels // 2
    for basis in range(basis_count):
        terms = dot(out_ref[basis], cot, TN)
        send_ref[basis] = terms[half:].astype(send_ref.dtype)
        keep_ref[basis] = terms[:half]


def mix_body(weight_ref, basis_ref, own_ref, pair_ref):
    basis_count, channels, outs = weight_ref.shape
    cells = own_ref.shape[0]
    source = jnp.concatenate([basis_ref[basis] for basis in range(basis_count)], axis=1)
    total = dot(source, weight_ref[...].reshape(basis_count * channels, outs))
    own_ref[...] = total[:cells]
    pair_ref[...] = total[cells:].astype(pair_ref.dtype)


def backward_body(lay, offsets, own_ref, pair_ref, near_ref, next_ref, core_ref, cross_ref, taps_ref, index_ref,
                  weight_ref, own_grad_ref, pair_grad_ref, ext_scr, basis_scr, band_scr, sum_scr):
    rows, cols, _ = own_ref.shape
    basis_count, channels, outs = weight_ref.shape
    odd = lay.odd()
    rim = (ext_scr.shape[1] - cols) // 2
    beside = outs // channels
    place_rows(
        ext_scr, lambda v: v, own_ref, pair_ref, near_ref, next_ref, core_ref, cross_ref,
        rows // beside * cols, 4 * (rows // beside) * rim,
    )
    weight = weight_ref[...].reshape(basis_count * channels, outs)
    first_row = (lax.axis_index("lat") - odd) * rows
    ext_rows, ext_cols, _ = ext_scr.shape
    blocks = ext_cols // TILE
    for row in range(ext_rows):
        basis_grad = dot(ext_scr[row], weight, NT).astype(bf16)
        low = row * basis_count * TILE
        for basis in range(basis_count):
            for block in range(blocks):
                piece = basis_grad[block * TILE : (block + 1) * TILE, basis * channels : (basis + 1) * channels]
                start = low + basis * TILE
                basis_scr[start : start + TILE, block * channels : (block + 1) * channels] = piece
        reached = [target + 2 * (offsets // 2) - row for target in range(2 * rows)]
        band_scr[low : low + basis_count * TILE, :] = bands(taps_ref, index_ref, first_row + row, basis_count, reached, offsets)
    sum_scr[...] = jnp.zeros(sum_scr.shape, f32)
    for block in range(0, blocks, 2):
        sides = min(2, blocks - block)
        spread = dot(band_scr[...], basis_scr[:, block * channels : (block + sides) * channels], TN)
        for target in range(2 * rows):
            for side in range(sides):
                start = (block + side) * TILE
                piece = spread[target * SLOT : (target + 1) * SLOT, side * channels : (side + 1) * channels]
                sum_scr[target, start : start + SLOT, :] = sum_scr[target, start : start + SLOT, :] + piece
    for row in range(rows):
        for ref, slot in ((own_grad_ref, odd * rows), (pair_grad_ref, (1 - odd) * rows)):
            ref[row * cols : (row + 1) * cols, :] = sum_scr[slot + row, TILE : TILE + cols, :].astype(bf16)


def finish_body(lay, own_ref, pair_ref, grad_ref):
    shape = (own_ref.shape[1], grad_ref.shape[1])
    place, column = lay.places(shape, 0), lax.broadcasted_iota(jnp.int32, shape, 1)
    odd = lay.odd()
    own = (column == lay.whole(place, odd)).astype(bf16)
    pair = (column == lay.whole(place, 1 - odd)).astype(bf16)
    grad_ref[...] = (dot(own_ref[...], own) + dot(pair_ref[...], pair)).astype(bf16)


def after(array, *others):
    return lax.optimization_barrier((array, *others))[0]


def swap(array, axis, stride):
    return lax.ppermute(array, axis, [(i, i ^ stride) for i in range(lax.axis_size(axis))])


def swap_across(array, axis, stride, wrap):
    size = lax.axis_size(axis)
    pairs = [(i, i + stride if i // stride % 2 else i - stride) for i in range(size)]
    return lax.ppermute(array, axis, [(i, j % size) for i, j in pairs if wrap or 0 <= j < size])


def flat(rows, width):
    wide = width // rows.shape[2]
    lines = [
        jnp.concatenate([rows[row + side] for side in range(wide)], axis=1) for row in range(0, rows.shape[0], wide)
    ]
    return jnp.concatenate(lines, axis=0)


def row_halo(own, pair, near_more):
    lat = lax.axis_index("lat")
    own_first = (lat & 1) != ((lat >> 1) & 1)
    width = own[1].shape[2]
    to_near = [flat(jnp.where(own_first, a, b), width) for a, b in zip(own, pair)]
    to_far = [flat(jnp.where(own_first, b, a), width) for a, b in zip(own, pair)]
    near = swap(jnp.concatenate([*to_near, *near_more], axis=0), "lat", 2)
    return near, swap_across(jnp.concatenate(to_far, axis=0), "lat", 2, False)


def edges(near, own, pair, far, rim):
    rows, cols, width = own[1].shape

    def at(first):
        fields, base = [], 0
        for a, b in zip(own, pair):
            lines = rows * a.shape[2] // width
            starts = [base + line * cols + first for line in range(lines)]
            kept = [flat(v[:, first : first + rim], width) for v in (a, b)]
            fields += [near[start : start + rim] for start in starts] + kept + [far[start : start + rim] for start in starts]
            base += lines * cols
        return jnp.concatenate(fields, axis=0)

    even = (lax.axis_index("lon") & 1) == 0
    left, right = at(0), at(cols - rim)
    return jnp.where(even, right, left), jnp.where(even, left, right)


def column_halo(lay, to_core, to_cross):
    cross = swap(to_cross, "lon", 3) if lay.merged else swap_across(to_cross, "lon", 1, True)
    return swap(to_core, "lon", 1), cross


def local(features, weight, tap_values, basis_index, half_width, cotangent):
    channels, rows, cols = features.shape
    basis_count = weight.shape[0]
    _, offsets, window = tap_values.shape
    rim = (window - 1) // 2
    lay = Layout(channels, lax.axis_size("lat"), lax.axis_size("lon"))
    odd = lay.odd()
    half = channels // 2

    split = features.reshape(half // lay.pair, 2, lay.pair * rows, cols)
    to_pair = lax.dynamic_index_in_dim(split, 1 - odd, 1, False).reshape(half * rows, cols)
    to_keep = lax.dynamic_index_in_dim(split, odd, 1, False).reshape(half, rows, cols)

    def channels_last(v):
        return jnp.transpose(v, (1, 2, 0))

    def from_pair(v):
        return channels_last(swap(v.reshape(-1, cols), "lat", 1).reshape(-1, rows, cols))

    pair_cot = from_pair(cotangent)
    pair = from_pair(to_pair), pair_cot
    mine = channels_last(to_keep), channels_last(cotangent)

    far = jnp.abs(jnp.arange(window) - rim)
    index = jnp.where(far[None, None, :] <= half_width[:, None, None], basis_index, -1)
    fill = ((rows, rows), (0, offsets % 2), (0, SLOT - window))
    index = jnp.pad(index, fill, constant_values=-1)
    taps = jnp.pad(tap_values.astype(f32), fill)

    full = weight.reshape(basis_count, lay.own, channels // lay.parts)
    for axis, flip, _ in lay.split:
        other = swap(full, axis, flip)
        low = (lax.axis_index(axis) // flip) % 2 == 0
        full = jnp.where(low, jnp.concatenate([full, other], 2), jnp.concatenate([other, full], 2))
    gather = list(reversed(lay.steps))

    def widen(full, step):
        return jnp.concatenate([full, swap(full, step[0], step[1])], axis=1)

    lot = basis_count * lay.own

    def tail(array, count):
        return [array[array.shape[0] - (i + 1) * lot : array.shape[0] - i * lot] for i in reversed(range(count))]

    own = [lax.optimization_barrier(weight.reshape(lot, channels))] if lay.merged else []
    near, far = row_halo(mine, pair, own)
    by_near = tail(near, len(own))
    to_core, to_cross = edges(near, mine, pair, far, rim)
    core, cross = column_halo(lay, to_core, to_cross)
    if lay.merged:
        held = jnp.concatenate(own + by_near, axis=0)
        held = [held, swap(after(held, to_core, to_cross), "lat", 4)]
    else:
        for step in gather[:-1]:
            full = widen(full, step)

    cells = rows * cols
    ext = (4 * rows, cols + 2 * rim)
    basis_out, send, keep = call(
        lambda *refs: forward_body(lay, offsets, *refs), "forward",
        [((basis_count, 2 * cells, half), bf16), ((basis_count, half // 2, channels), f32),
         ((basis_count, half // 2, channels), f32)],
        mine[0], pair[0], near, far, core, cross, taps, index, mine[1], pair[1],
        scratch=[pltpu.VMEM((*ext, half), bf16)],
    )
    for rank, (axis, flip, _) in enumerate(lay.steps):
        terms = (keep, swap(send, axis, flip))
        if rank == 2:
            terms = (keep, after(terms[1], own_grad))
        elif rank == 0:
            if lay.merged:
                held = [after(v, send) for v in held]
                (first, third), (second, fourth) = ((v[:lot], v[lot:]) for v in held)
                held = jnp.concatenate([first, second, third, fourth], axis=0)
                other = swap(held, "lon", 3)
        elif rank == 1:
            if lay.merged:
                other = after(other, send)
                blocks = [v[i * lot : (i + 1) * lot] for v, i in ((held, 0), (held, 1), (other, 0), (other, 1),
                                                                  (held, 2), (held, 3), (other, 2), (other, 3))]
                full = jnp.concatenate([v.reshape(basis_count, lay.own, channels) for v in blocks], axis=1)
            full = widen(full, gather[-1])
            own_out, pair_out = call(
                mix_body, "mix", [((cells, channels), f32), ((cells, channels), bf16)], full, basis_out
            )
            mine_after = after(mine[1], pair_out)
            pair_out = swap(pair_out, "lat", 1)
            own_grad, pair_grad = call(
                lambda *refs: backward_body(lay, offsets, *refs), "backward",
                [((cells, half), bf16), ((cells, half), bf16)],
                mine_after, pair[1], near, far, core, cross, taps, index, full,
                scratch=[pltpu.VMEM((*ext, channels), bf16),
                         pltpu.VMEM((ext[0] * basis_count * TILE, ext[1] // TILE * half), bf16),
                         pltpu.VMEM((ext[0] * basis_count * TILE, 2 * rows * SLOT), bf16),
                         pltpu.VMEM((2 * rows, ext[1] + TILE, half), f32)],
            )
            pair_grad = swap(pair_grad, "lat", 1)
        if rank + 1 < len(lay.steps):
            size = keep.shape[1] // 2
            send = (terms[0][:, size:] + terms[1][:, size:]).astype(bf16 if rank < 3 else f32)
            keep = terms[0][:, :size] + terms[1][:, :size]
    output = (own_out + pair_out).astype(bf16)
    (input_grad,) = call(
        lambda *refs: finish_body(lay, *refs), "finish", [((cells, channels), bf16)], own_grad, pair_grad
    )

    def channels_first(v):
        return jnp.transpose(v.reshape(rows, cols, channels), (2, 0, 1))

    output, input_grad = channels_first(output), channels_first(input_grad)
    grad = terms[0] + after(terms[1], output, input_grad)
    for axis, flip, _ in reversed(lay.split):
        size = grad.shape[2] // 2
        odd_part = (lax.axis_index(axis) // flip) % 2
        other = swap(lax.dynamic_slice_in_dim(grad, (1 - odd_part) * size, size, 2), axis, flip)
        grad = lax.dynamic_slice_in_dim(grad, odd_part * size, size, 2) + other
    weight_grad = grad.reshape(basis_count, weight.shape[1])

    return output, input_grad, weight_grad


def solution(mesh):
    field = P(None, "lat", "lon")
    flat = P(None, ("lat", "lon"))
    return jax.shard_map(
        local,
        mesh=mesh,
        in_specs=(field, flat, P(), P(), P(), field),
        out_specs=(field, field, flat),
        check_vma=False,
    )
```
